32 devices in a mesh: own: 8 (over z, y), rep: 4 (over x, core).
Axes of the slice: x: 2, y: 2, z: 4, core: 2. Of those that a mesh axis runs over, the one named last changes fastest.
Arguments:
- hidden: bfloat16 [1024, 1024], P('own', 'rep'), may hold values from -140 to 140
- weight: bfloat16 [8, 2048, 1024], P('own', None, 'rep'), may hold values from -0.1875 to 0.1875
- bucket_map: int32 [8], replicated, may hold values from 0 to 7, each once
- active: int32 [1024, 2], P('own'), may hold values from 0 to 7, all different within a row; in each aligned block of 128 rows (0 to 127, 128 to 255, ...) at most 64 rows name the same one
- label_pick: int32 [1024], P('own'), may hold values from 0 to 4095
Outputs:
- sample_loss: float32 [1024], P('own')
- grad_hidden: float32 [1024, 1024], P('own', 'rep')
- grad_weight: bfloat16 [8, 2048, 1024], P('own', None, 'rep')
The draws below stay inside these ranges and needn't reach their ends.
Inputs may be any that keep to these rules, and one draw needn't show every extreme that they name: `bucket_map`: each weight slot is named once. `active`: A sample's 2 bucket ids differ. Among the 128 samples of one index of own, no bucket is named by more than 64 samples, a bound that some block reaches.
All inputs are finite; a program needn't handle non-finite values.
Results may differ from the reference program's by a relative error of at most 0.0032.
Values may be sent and summed in bfloat16 or wider, within the bound.
A program may use at most 64 MiB of HBM per device.

```python
import math
import jax
import jax.numpy as jnp
import numpy as np
from jax import lax

D = 1024
LB = 2048
K = 2
SAMP_DEV = 128
BUCKETS = 8
SAMPLES = 1024
MOST = 64
CAP_BUCKET = 512


def draw_hidden(key, part):
    first_key = jax.random.fold_in(key, 0)
    return (3.0 * jax.random.truncated_normal(first_key, -6.0, 6.0, (SAMPLES, D), jnp.float32)).astype(jnp.bfloat16)


def place_ends(drawn, rng, least, largest):
    dims = drawn.shape
    index_at = [jax.random.randint(jax.random.fold_in(rng, axis), (), 0, dims[axis]) for axis in range(len(dims))]
    drawn = drawn.at[tuple(index_at)].set(least)
    longest = dims.index(max(dims))
    index_at[longest] = (index_at[longest] + 1) % dims[longest]
    return drawn.at[tuple(index_at)].set(largest)


def shard_levels(rng, shape, shards, least, high):
    def one(position, parts):
        draws = jax.random.uniform(jax.random.fold_in(jax.random.fold_in(rng, 6), position), (parts,), jnp.float32, least / len(shards), high / len(shards))
        return jnp.repeat(jnp.exp(draws), shape[position] // parts).reshape((-1,) + (1,) * (len(shape) - position - 1))

    loudness = one(*shards[0])
    for cut in shards[1:]:
        loudness = loudness * one(*cut)
    return loudness


def routed_block(rng, own, number, rows, count, top, most, skew):
    order = jax.random.permutation(rng, count)
    heavy_load, usual = shares(count, rows * top, most, skew, True), shares(count, rows * top, most, skew, False)
    places = jnp.arange(count)

    def named(lengths, rotation):
        used = int((lengths > 0).sum())
        fixed = max(1, used // 4)
        passed = fixed + (places - fixed + rotation * (used - fixed)) % max(1, count - fixed)
        return jnp.zeros((count,), jnp.int32).at[order[jnp.where(places < fixed, places, passed)]].set(jnp.asarray(lengths, jnp.int32))

    lengths = jnp.where(number % 4 == 0, named(heavy_load, number // 4), named(usual, number - number // 4 - 1))
    mixed = jax.random.permutation(jax.random.fold_in(own, 3), count)
    donor, receiver = mixed[0:count // 2 * 2:2], mixed[1:count // 2 * 2:2]
    slack = jnp.minimum(lengths[donor] - 1, most - lengths[receiver]) // 2
    slack = jnp.where((donor == order[0]) | (receiver == order[0]) | (lengths[receiver] == 0), 0, jnp.maximum(slack, 0))
    passed = jax.random.randint(jax.random.fold_in(own, 4), (count // 2,), 0, 1 << 20) % (slack + 1)
    lengths = lengths.at[donor].add(-passed).at[receiver].add(passed)
    labels = jnp.searchsorted(jnp.cumsum(lengths), jnp.arange(rows * top), side="right").astype(jnp.int32)
    listing = labels.reshape(top, rows).T
    listing = listing[jax.random.permutation(jax.random.fold_in(own, 1), rows)]
    rotation = jax.random.randint(jax.random.fold_in(own, 2), (rows, 1), 0, top)
    return jnp.take_along_axis(listing, (jnp.arange(top)[None, :] + rotation) % top, axis=1)


def shares(amount, total, limit, skew, full):
    loads = [(1 << 20) // math.isqrt(grade ** skew) + 1 for grade in range(1, amount + 1)]
    largest = limit if full else min(limit, max(-(-total // amount), total * loads[0] // sum(loads)))
    least = 1 if total - largest >= amount - 1 else 0
    given, surplus = [largest] + [least] * (amount - 1), total - largest - least * (amount - 1)
    while surplus > 0:
        candidates = [i for i in range(1, amount) if given[i] < largest] or [i for i in range(1, amount) if given[i] < limit]
        whole, remaining = sum([loads[i] for i in candidates]), surplus
        for i in candidates:
            addition = min(limit - given[i], max(1, remaining * loads[i] // whole), surplus)
            given[i] = given[i] + addition
            surplus = surplus - addition
    return np.array(given)


def bell_draw(own_key, shape, width, limit, cuts=(), kind=jnp.bfloat16):
    array = jax.random.normal(own_key, shape, jnp.float32) * width
    if len(cuts) > 0:
        array = shard_levels(own_key, shape, cuts, -0.22, 0.18) * array
    return jnp.clip(array, min=-limit, max=limit).astype(kind)


def setup_inputs(seed: int = 0) -> dict:
    keys = jax.random.split(jax.random.key(seed), 6)
    hidden = draw_hidden(jax.random.fold_in(keys[5], 71), 0)
    weight = bell_draw(keys[1], (BUCKETS, LB, D), D ** -0.5, 0.1875, ((0, 8), (2, 4)))
    bucket_map = jax.random.permutation(keys[2], BUCKETS).astype(jnp.int32)
    active_keys = jax.random.split(jax.random.fold_in(keys[3], 1), SAMPLES // SAMP_DEV)
    active_turns = jax.random.permutation(jax.random.fold_in(keys[3], 3), SAMPLES // SAMP_DEV)
    active = jax.vmap(lambda own, number: routed_block(jax.random.fold_in(keys[3], 2), own, number, SAMP_DEV, BUCKETS, K, MOST, 2))(active_keys, active_turns).reshape((SAMPLES, K))
    label_pick = place_ends(jax.random.randint(keys[4], (SAMPLES,), 0, K * LB), jax.random.fold_in(keys[4], 1), 0, (K * LB) - 1).astype(jnp.int32)
    return {"hidden": hidden, "weight": weight, "bucket_map": bucket_map, "active": active, "label_pick": label_pick}


def reference(hidden, weight, bucket_map, active, label_pick):
    pair_count = SAMPLES * K
    slot_index = bucket_map[active].reshape(pair_count).astype(jnp.int32)
    pair_index = jnp.arange(pair_count, dtype=jnp.int32)
    sample_of = pair_index // K
    pick_value = label_pick[sample_of]
    target_col = jnp.where(pick_value // LB == pair_index % K, pick_value % LB, -1).astype(jnp.int32)
    order_pairs = jnp.argsort(slot_index, stable=True).astype(jnp.int32)
    counts = jax.ops.segment_sum(jnp.ones((pair_count,), jnp.int32), slot_index, BUCKETS)
    starts = (jnp.cumsum(counts) - counts).astype(jnp.int32)
    order_padded = jnp.concatenate([order_pairs, jnp.zeros((CAP_BUCKET,), jnp.int32)])
    columns = jnp.arange(LB, dtype=jnp.int32)[None, :]
    local_rows = jnp.arange(CAP_BUCKET, dtype=jnp.int32)

    def rows_of(bucket):
        picked = lax.dynamic_slice(order_padded, (starts[bucket],), (CAP_BUCKET,)).astype(jnp.int32)
        valid = local_rows < counts[bucket]
        gathered = jnp.where(valid[:, None], hidden[sample_of[picked]], jnp.zeros((), jnp.bfloat16))
        logits = jnp.dot(gathered, weight[bucket].T, preferred_element_type=jnp.float32)
        return picked, valid, gathered, logits

    def stats_of(bucket):
        picked, valid, gathered, logits = rows_of(bucket)
        row_max = jnp.max(logits, axis=1)
        row_sum = jnp.sum(jnp.exp(logits - row_max[:, None]), axis=1)
        row_target = jnp.sum(jnp.where(columns == target_col[picked][:, None], logits, 0.0), axis=1)
        dest = jnp.where(valid, picked, pair_count)
        return dest, row_max, row_sum, row_target

    dest, row_max, row_sum, row_target = lax.map(stats_of, jnp.arange(BUCKETS, dtype=jnp.int32))
    dest = dest.reshape(-1)
    pair_max = jnp.zeros((pair_count,), jnp.float32).at[dest].set(row_max.reshape(-1), mode="drop")
    pair_sum = jnp.zeros((pair_count,), jnp.float32).at[dest].set(row_sum.reshape(-1), mode="drop")
    pair_target = jnp.zeros((pair_count,), jnp.float32).at[dest].set(row_target.reshape(-1), mode="drop")
    pair_max = pair_max.reshape(SAMPLES, K)
    peak_max = jnp.max(pair_max, axis=1)
    norm_sum = jnp.sum(pair_sum.reshape(SAMPLES, K) * jnp.exp(pair_max - peak_max[:, None]), axis=1)
    log_norm = peak_max + jnp.log(norm_sum)
    sample_loss = log_norm - jnp.sum(pair_target.reshape(SAMPLES, K), axis=1)
    pair_norm = jnp.repeat(log_norm, K)

    def grads_of(carry, bucket):
        picked, valid, gathered, logits = rows_of(bucket)
        onehot = (columns == target_col[picked][:, None]).astype(jnp.float32)
        grad_logits = jnp.exp(logits - pair_norm[picked][:, None]) - onehot
        grad_logits = jnp.where(valid[:, None], grad_logits, 0.0).astype(jnp.bfloat16)
        block_grad = jnp.dot(grad_logits.T, gathered, preferred_element_type=jnp.float32).astype(jnp.bfloat16)
        row_grads = jnp.dot(grad_logits, weight[bucket], preferred_element_type=jnp.float32)
        sample_dest = jnp.where(valid, sample_of[picked], SAMPLES)
        carry = carry.at[sample_dest].add(row_grads, mode="drop")
        return carry, block_grad

    grad_hidden, grad_weight = lax.scan(grads_of, jnp.zeros((SAMPLES, D), jnp.float32), jnp.arange(BUCKETS, dtype=jnp.int32))
    return sample_loss, grad_hidden, grad_weight
```

```python
import functools
import jax
import jax.numpy as jnp
from jax import lax
from jax.experimental import pallas as pl
from jax.experimental.pallas import tpu as pltpu
from jax.sharding import PartitionSpec as P

MESH = pl.DeviceIdType.MESH
F32 = jnp.float32
BF16 = jnp.bfloat16
NT = (((1,), (1,)), ((), ()))
TN = (((0,), (0,)), ((), ()))


def ranks(slot0, slot1, buckets, upper):
    sources, samples = slot0.shape
    bucket = lax.broadcasted_iota(jnp.int32, (buckets, samples), 0)
    hits = [
        jnp.where((slot0[s : s + 1] == bucket) | (slot1[s : s + 1] == bucket), 1.0, 0.0)
        for s in range(sources)
    ]
    hits = jnp.concatenate(hits, axis=0) if sources > 1 else hits[0]
    earlier = jnp.dot(hits.astype(BF16), upper, preferred_element_type=F32)
    return jnp.where(hits > 0.5, earlier, -1.0).astype(jnp.int32)


def lane_pick(values, index):
    return jnp.take_along_axis(values, index, axis=1)


def kernel(
    n, depth, picks_labels, bmap, meta, hidden, weight,
    loss_ref, gh_ref, gw_ref,
    metas, wfull, sendbuf, rows, rinfo, lt, stats, statrep, comb, statown, norms, tsums,
    g_all, gh_acc, ghsend, ghrecv,
    s_meta, r_meta, s_w, r_w, s_row, r_row, s_fx, r_fx, s_fc, r_fc, s_fr, r_fr,
    s_sr, r_sr, s_so, r_so, s_gx, r_gx, s_gc, r_gc, s_gr, r_gr, s_gh, r_gh,
):
    o = lax.axis_index("own")
    r = lax.axis_index("rep")
    p1 = r + 1 - 2 * lax.rem(r, 2)
    p2 = lax.rem(r + 2, 4)
    p3 = lax.rem(p1 + 2, 4)
    labels, part = weight.shape
    samples = hidden.shape[0]
    cols = labels // 4
    row_count = n * depth
    pending = []

    def send(src, dst, ssem, rsem, own, rep):
        copy = pltpu.make_async_remote_copy(
            src_ref=src, dst_ref=dst, send_sem=ssem, recv_sem=rsem,
            device_id={"own": own, "rep": rep}, device_id_type=MESH,
        )
        copy.start()
        pending.append(copy)
        return copy

    def at_rows(s):
        return pl.ds(pl.multiple_of(s * depth, depth), depth)

    def at_part(q):
        return pl.ds(pl.multiple_of(q * part, part), part)

    def at_cols(q, c=0, size=None):
        size = cols if size is None else size
        return pl.ds(pl.multiple_of(q * cols + c * size, size), size)

    barrier = pltpu.get_barrier_semaphore()
    for k in range(1, n):
        pl.semaphore_signal(barrier, inc=1, device_id={"own": lax.rem(o + k, n), "rep": r}, device_id_type=MESH)
    for q in (p1, p2, p3):
        pl.semaphore_signal(barrier, inc=1, device_id={"own": o, "rep": q}, device_id_type=MESH)
    pl.semaphore_wait(barrier, n - 1 + 3)

    w_copies = [
        send(weight.at[at_cols(q)], wfull.at[:, at_part(r)], s_w.at[i], r_w.at[i], o, q)
        for i, q in ((1, p2), (2, p3), (0, p1))
    ]
    meta_copies = [
        send(meta, metas.at[o], s_meta.at[k - 1], r_meta.at[k - 1], lax.rem(o + k, n), r)
        for k in range(1, n)
    ]

    below = lax.broadcasted_iota(jnp.int32, (samples, samples), 0)
    right = lax.broadcasted_iota(jnp.int32, (samples, samples), 1)
    upper = jnp.where(below < right, 1.0, 0.0).astype(BF16)

    def slots(ids):
        out = jnp.zeros_like(ids)
        for b in range(n):
            out = jnp.where(ids == b, bmap[b], out)
        return out

    mine = meta[...]
    own_rank = ranks(slots(mine[0:1]), slots(mine[1:2]), n, upper)
    place = lax.broadcasted_iota(jnp.int32, (depth, samples), 0)
    pack = jnp.concatenate(
        [jnp.where(own_rank[b : b + 1] == place, 1.0, 0.0).astype(BF16) for b in range(n)], axis=0
    )
    packed = jnp.dot(pack, hidden[...], preferred_element_type=F32).astype(BF16)
    for b in range(n):
        sendbuf[b] = packed[b * depth : (b + 1) * depth]
    row_copies = [
        send(sendbuf.at[lax.rem(o + k, n)], rows.at[at_rows(o), at_part(r)], s_row.at[k - 1], r_row.at[k - 1], lax.rem(o + k, n), r)
        for k in range(1, n)
    ]
    rows[at_rows(o), at_part(r)] = sendbuf[o]
    wfull[:, at_part(r)] = weight[at_cols(r), :]
    metas[o] = mine

    fx, fc, fr = [], [], []
    for k in range(n):
        s = lax.rem(o - k + n, n)
        if k > 0:
            row_copies[k - 1].wait_recv()
        block = rows.at[at_rows(s), at_part(r)]
        fx.append(send(block, block, s_fx.at[k], r_fx.at[k], o, p2))
        fc.append(send(block, block, s_fc.at[k], r_fc.at[k], o, p1))

    for c in meta_copies:
        c.wait_recv()
    slot0 = slots(metas[:, 0, :])
    slot1 = slots(metas[:, 1, :])
    pick = metas[:, 2, :]
    rank_all = ranks(slot0, slot1, n, upper)
    wanted = jnp.where(pick < labels, slot0, slot1)
    code = jnp.where(wanted == o, jnp.where(pick < labels, pick, pick - labels) + 1, 0)
    code_hi = (code // 64).astype(F32)
    code_lo = (code - (code // 64) * 64).astype(F32)
    lane = lax.broadcasted_iota(jnp.int32, (1, samples), 1)
    sub = lax.broadcasted_iota(jnp.int32, (8, samples), 0)
    bucket_sub = lax.broadcasted_iota(jnp.int32, (n, samples), 0)
    infos = []
    place2 = lax.broadcasted_iota(jnp.int32, (2 * depth, samples), 0)
    for sp in range(n // 2):
        info = jnp.zeros((8, 2 * depth), F32)
        for h in range(2):
            s = 2 * sp + h
            rank_me = jnp.max(
                jnp.where(bucket_sub == o, rank_all[s * n : (s + 1) * n], -1), axis=0, keepdims=True
            )
            member = jnp.where(
                (rank_me >= 0) & (rank_me + h * depth == place2), 1.0, 0.0
            ).astype(BF16)
            facts = jnp.where(
                sub == 0, lane.astype(F32),
                jnp.where(sub == 1, code_hi[s : s + 1], jnp.where(sub == 2, code_lo[s : s + 1], jnp.where(sub == 3, 1.0, 0.0))),
            ).astype(BF16)
            info = info + lax.dot_general(facts, member, NT, preferred_element_type=F32)
        infos.append(info)
    row_index = [x[0:1].astype(jnp.int32) for x in infos]
    row_valid = jnp.concatenate([x[3:4] for x in infos], axis=1) > 0.5
    row_target = jnp.concatenate([(x[1:2] * 64.0 + x[2:3]) for x in infos], axis=1).astype(jnp.int32) - 1

    for k in range(n):
        fx[k].wait_recv()
        s = lax.rem(o - k + n, n)
        block = rows.at[at_rows(s), at_part(p2)]
        fr.append(send(block, block, s_fr.at[k], r_fr.at[k], o, p1))
    for k in range(n):
        fc[k].wait_recv()
    for c in w_copies:
        c.wait_recv()
    for k in range(n):
        fr[k].wait_recv()

    logits = lax.dot_general(wfull[...], rows[...], NT, preferred_element_type=F32)
    top = jnp.max(logits, axis=0, keepdims=True)
    label_id = lax.broadcasted_iota(jnp.int32, (cols, row_count), 0) + r * cols
    hot = label_id == row_target
    target_sum = jnp.sum(jnp.where(hot, logits, 0.0), axis=0, keepdims=True)
    raised = jnp.exp(logits - top)
    lt[...] = raised
    lse = top + jnp.log(jnp.sum(raised, axis=0, keepdims=True))
    for sp in range(n // 2):
        stats[sp : sp + 1, :] = lse[:, sp * 128 : (sp + 1) * 128]
        stats[n // 2 + sp : n // 2 + sp + 1, :] = target_sum[:, sp * 128 : (sp + 1) * 128]
    sr = [
        send(stats, statrep.at[r], s_sr.at[i], r_sr.at[i], o, q)
        for i, q in ((1, p2), (2, p3), (0, p1))
    ]
    statrep[r] = stats[...]
    for c in sr:
        c.wait_recv()
    parts = [statrep[q] for q in range(4)]
    high = jnp.maximum(jnp.maximum(parts[0], parts[1]), jnp.maximum(parts[2], parts[3]))
    total = high + jnp.log(sum(jnp.exp(x - high) for x in parts))
    is_lse = lax.broadcasted_iota(jnp.int32, (n, samples), 0) < n // 2
    comb[...] = jnp.where(is_lse, total, sum(parts))
    so = [
        send(comb, statown.at[o], s_so.at[k - 1], r_so.at[k - 1], lax.rem(o + k, n), r)
        for k in range(1, n)
    ]
    statown[o] = comb[...]
    for c in so:
        c.wait_recv()
    norm_rows = []
    for sp in range(n // 2):
        held = statown[:, sp, :]
        pair = []
        for h in range(2):
            s = 2 * sp + h
            rank = rank_all[s * n : (s + 1) * n]
            index = jnp.where(rank >= 0, rank + h * depth, 0)
            value = jnp.where(rank >= 0, lane_pick(held, index), -3.0e38)
            most = jnp.max(value, axis=0, keepdims=True)
            norm = most + jnp.log(jnp.sum(jnp.exp(value - most), axis=0, keepdims=True))
            norms[s : s + 1, :] = norm
            pair.append(
                lane_pick(jnp.broadcast_to(norm, (8, samples)), jnp.broadcast_to(row_index[sp], (8, samples)))[0:1]
            )
        norm_rows.append(jnp.where(lane < depth, pair[0], pair[1]))
    row_norm = jnp.concatenate(norm_rows, axis=1)
    scale = jnp.where(row_valid, jnp.exp(top - row_norm), 0.0)

    chunk = cols // 4
    gx, gc, gr = [], [], []
    for c in range(4):
        ids = lax.broadcasted_iota(jnp.int32, (chunk, row_count), 0) + (r * cols + c * chunk)
        grad = lt[c * chunk : (c + 1) * chunk, :] * scale - jnp.where(ids == row_target, 1.0, 0.0)
        g_all[at_cols(r, c, chunk), :] = grad.astype(BF16)
        block = g_all.at[at_cols(r, c, chunk)]
        gx.append(send(block, block, s_gx.at[c], r_gx.at[c], o, p2))
        gc.append(send(block, block, s_gc.at[c], r_gc.at[c], o, p1))

    for sp in range(n // 2):
        held = statown[:, n // 2 + sp, :]
        for h in range(2):
            s = 2 * sp + h
            rank = rank_all[s * n : (s + 1) * n]
            index = jnp.where(rank >= 0, rank + h * depth, 0)
            value = jnp.where(rank >= 0, lane_pick(held, index), 0.0)
            tsums[s : s + 1, :] = jnp.sum(value, axis=0, keepdims=True)
    loss_ref[...] = norms[pl.ds(o, 1), :] - tsums[pl.ds(o, 1), :]

    def row_term(q):
        return lax.dot_general(g_all[at_cols(q), :], weight[at_cols(q), :], TN, preferred_element_type=F32)

    def weight_term(q):
        gw_ref[at_cols(q), :] = jnp.dot(
            g_all[at_cols(q), :], rows[:, at_part(r)], preferred_element_type=F32
        ).astype(BF16)

    gh_acc[...] = row_term(r)
    weight_term(r)
    for c in range(4):
        gx[c].wait_recv()
        block = g_all.at[at_cols(p2, c, chunk)]
        gr.append(send(block, block, s_gr.at[c], r_gr.at[c], o, p1))
    for c in range(4):
        gc[c].wait_recv()
    gh_acc[...] += row_term(p1)
    gh_acc[...] += row_term(p2)
    for c in range(4):
        gr[c].wait_recv()
    ghsend[...] = (gh_acc[...] + row_term(p3)).astype(BF16)
    back = [
        send(ghsend.at[at_rows(lax.rem(o + k, n))], ghrecv.at[at_rows(o)], s_gh.at[k - 1], r_gh.at[k - 1], lax.rem(o + k, n), r)
        for k in range(1, n)
    ]
    ghrecv[at_rows(o), :] = ghsend[at_rows(o), :]
    weight_term(p1)
    weight_term(p2)
    weight_term(p3)
    for c in back:
        c.wait_recv()
    gh_ref[...] = lax.dot_general(pack, ghrecv[...], TN, preferred_element_type=F32)
    for c in pending:
        c.wait_send()


def fused(hidden, weight, bucket_map, active, label_pick):
    samples, part = hidden.shape
    labels = weight.shape[1]
    n = bucket_map.shape[0]
    depth = 2 * samples * active.shape[1] // n
    cols = labels // 4
    row_count = n * depth
    meta = jnp.concatenate(
        [active.T, label_pick[None], jnp.zeros((5, samples), jnp.int32)], axis=0
    )
    vmem = pl.BlockSpec(memory_space=pltpu.VMEM)
    dma = pltpu.SemaphoreType.DMA
    sems = []
    for count in (n - 1, 3, n - 1, n, n, n, 3, n - 1, 4, 4, 4, n - 1):
        sems += [dma((count,)), dma((count,))]
    loss, grad_hidden, grad_weight = pl.pallas_call(
        functools.partial(kernel, n, depth, labels),
        out_shape=(
            jax.ShapeDtypeStruct((1, samples), F32),
            jax.ShapeDtypeStruct((samples, part), F32),
            jax.ShapeDtypeStruct((labels, part), BF16),
        ),
        in_specs=[pl.BlockSpec(memory_space=pltpu.SMEM), vmem, vmem, vmem],
        out_specs=(vmem, vmem, vmem),
        scratch_shapes=[
            pltpu.VMEM((n, 8, samples), jnp.int32),
            pltpu.VMEM((cols, 4 * part), BF16),
            pltpu.VMEM((n, depth, part), BF16),
            pltpu.VMEM((row_count, 4 * part), BF16),
            pltpu.VMEM((8, row_count), F32),
            pltpu.VMEM((cols, row_count), F32),
            pltpu.VMEM((n, samples), F32),
            pltpu.VMEM((4, n, samples), F32),
            pltpu.VMEM((n, samples), F32),
            pltpu.VMEM((n, n, samples), F32),
            pltpu.VMEM((n, samples), F32),
            pltpu.VMEM((n, samples), F32),
            pltpu.VMEM((labels, row_count), BF16),
            pltpu.VMEM((row_count, part), F32),
            pltpu.VMEM((row_count, part), BF16),
            pltpu.VMEM((row_count, part), BF16),
        ] + sems,
        compiler_params=pltpu.CompilerParams(
            collective_id=0, has_side_effects=True, vmem_limit_bytes=48 * 1024 * 1024
        ),
    )(bucket_map, meta, hidden, weight[0])
    return loss[0], grad_hidden, grad_weight[None]


def body(hidden, weight, bucket_map, active, label_pick):
    samp_count = hidden.shape[0]
    bucket_dev, label_count, feature_part = weight.shape
    picks = active.shape[1]
    bucket_total = bucket_map.shape[0]
    owner_count = lax.axis_size("own")
    slot_depth = max(2, 2 * samp_count * picks // bucket_total)
    pair_count = samp_count * picks
    slots_total = bucket_total * slot_depth
    row_count = owner_count * slot_depth
    pair_bucket = active.reshape(pair_count)
    bucket_iota = lax.broadcasted_iota(jnp.int32, (pair_count, bucket_total), 1)
    slot_index = jnp.sum(
        jnp.where(pair_bucket[:, None] == bucket_iota, bucket_map[None, :], 0), axis=1
    )
    slot_hits = (slot_index[:, None] == bucket_iota).astype(jnp.int32)
    earlier = jnp.cumsum(slot_hits, axis=0) - slot_hits
    rank_within = jnp.sum(earlier * slot_hits, axis=1)
    position = slot_index * slot_depth + rank_within
    pair_index = jnp.arange(pair_count, dtype=jnp.int32)
    pick_value = jnp.repeat(label_pick, picks)
    target_pair = jnp.where(
        pick_value // label_count == pair_index % picks, pick_value % label_count, -1
    )
    width_sent = hidden.shape[1]
    pair_rows = jnp.repeat(hidden, picks, axis=0)
    send_rows = jnp.zeros((slots_total, width_sent), jnp.bfloat16).at[position].set(pair_rows)
    send_target = jnp.full((slots_total,), -1, jnp.int32).at[position].set(target_pair)
    got_rows, got_target = (
        lax.all_to_all(
            send_rows.reshape(owner_count, bucket_dev * slot_depth, width_sent),
            "own",
            split_axis=0,
            concat_axis=0,
            tiled=True,
        ),
        lax.all_to_all(
            send_target.reshape(owner_count, bucket_dev * slot_depth),
            "own",
            split_axis=0,
            concat_axis=0,
            tiled=True,
        ),
    )
    received = got_rows.reshape(owner_count, bucket_dev, slot_depth, width_sent).transpose(
        1, 0, 2, 3
    )
    received = received.reshape(bucket_dev, row_count, width_sent)
    target_col = (
        got_target.reshape(owner_count, bucket_dev, slot_depth)
        .transpose(1, 0, 2)
        .reshape(bucket_dev, row_count)
    )
    partial_value = jnp.einsum("brd,bcd->brc", received, weight, preferred_element_type=jnp.float32)
    logits = lax.psum(partial_value, "rep")
    columns = lax.broadcasted_iota(jnp.int32, (1, 1, label_count), 2)
    row_max = jnp.max(logits, axis=2)
    row_sum = jnp.sum(jnp.exp(logits - row_max[..., None]), axis=2)
    row_target = jnp.sum(jnp.where(columns == target_col[..., None], logits, 0.0), axis=2)

    def to_sources(values):
        return (
            values.reshape(bucket_dev, owner_count, slot_depth)
            .transpose(1, 0, 2)
            .reshape(owner_count, bucket_dev * slot_depth)
        )

    back_max, back_sum, back_target = (
        lax.all_to_all(to_sources(row_max), "own", split_axis=0, concat_axis=0, tiled=True),
        lax.all_to_all(to_sources(row_sum), "own", split_axis=0, concat_axis=0, tiled=True),
        lax.all_to_all(to_sources(row_target), "own", split_axis=0, concat_axis=0, tiled=True),
    )
    pair_max = back_max.reshape(slots_total)[position].reshape(samp_count, picks)
    pair_sum = back_sum.reshape(slots_total)[position].reshape(samp_count, picks)
    pair_target = back_target.reshape(slots_total)[position].reshape(samp_count, picks)
    peak_max = jnp.max(pair_max, axis=1)
    norm_sum = jnp.sum(pair_sum * jnp.exp(pair_max - peak_max[:, None]), axis=1)
    log_norm = peak_max + jnp.log(norm_sum)
    sample_loss = log_norm - jnp.sum(pair_target, axis=1)
    send_norm = jnp.zeros((slots_total,), jnp.float32).at[position].set(jnp.repeat(log_norm, picks))
    got_norm = lax.all_to_all(
        send_norm.reshape(owner_count, bucket_dev * slot_depth),
        "own",
        split_axis=0,
        concat_axis=0,
        tiled=True,
    )
    row_norm = (
        got_norm.reshape(owner_count, bucket_dev, slot_depth)
        .transpose(1, 0, 2)
        .reshape(bucket_dev, row_count)
    )
    onehot = (columns == target_col[..., None]).astype(jnp.float32)
    grad_logits = (jnp.exp(logits - row_norm[..., None]) - onehot).astype(jnp.bfloat16)
    grad_weight = jnp.einsum(
        "brc,brd->bcd", grad_logits, received, preferred_element_type=jnp.float32
    ).astype(jnp.bfloat16)
    row_grads = jnp.einsum("brc,bcd->brd", grad_logits, weight, preferred_element_type=jnp.float32)
    send_grads = row_grads.reshape(bucket_dev, owner_count, slot_depth, feature_part).transpose(
        1, 0, 2, 3
    )
    send_grads = send_grads.reshape(owner_count, bucket_dev * slot_depth, feature_part)
    got_grads = lax.all_to_all(send_grads, "own", split_axis=0, concat_axis=0, tiled=True)
    pair_grads = got_grads.reshape(slots_total, feature_part)[position].reshape(
        samp_count, picks, feature_part
    )
    grad_hidden = jnp.sum(pair_grads, axis=1)
    return (sample_loss, grad_hidden, grad_weight)


def choose(hidden, weight, bucket_map, active, label_pick):
    samples, picks = active.shape
    buckets = bucket_map.shape[0]
    depth = 2 * samples * picks // buckets
    fits = (
        weight.shape[0] == 1
        and lax.axis_size("rep") == 4
        and buckets == 8
        and picks == 2
        and samples == 128
        and 2 * depth == samples
        and weight.shape[1] % 512 == 0
        and hidden.shape[1] % 128 == 0
    )
    run = fused if fits else body
    return run(hidden, weight, bucket_map, active, label_pick)


def solution(mesh):
    in_specs = (P("own", "rep"), P("own", None, "rep"), P(), P("own", None), P("own"))
    out_specs = (P("own"), P("own", "rep"), P("own", None, "rep"))
    return jax.shard_map(choose, mesh=mesh, in_specs=in_specs, out_specs=out_specs, check_vma=False)
```

```python
import functools
import jax
import jax.numpy as jnp
from jax import lax
from jax.experimental import pallas as pl
from jax.experimental.pallas import tpu as pltpu
from jax.sharding import PartitionSpec as P

MESH = pl.DeviceIdType.MESH
F32 = jnp.float32
BF16 = jnp.bfloat16
NT = (((1,), (1,)), ((), ()))
TN = (((0,), (0,)), ((), ()))


def ranks(slot0, slot1, buckets, upper):
    sources, samples = slot0.shape
    bucket = lax.broadcasted_iota(jnp.int32, (buckets, samples), 0)
    hits = [
        jnp.where((slot0[s : s + 1] == bucket) | (slot1[s : s + 1] == bucket), 1.0, 0.0)
        for s in range(sources)
    ]
    hits = jnp.concatenate(hits, axis=0) if sources > 1 else hits[0]
    earlier = jnp.dot(hits.astype(BF16), upper, preferred_element_type=F32)
    return jnp.where(hits > 0.5, earlier, -1.0).astype(jnp.int32)


def lane_pick(values, index):
    return jnp.take_along_axis(values, index, axis=1)


def kernel(
    n, depth, meta_hbm, hidden_hbm, weight_hbm,
    loss_ref, gh_ref, gw_hbm,
    meta, hidden, hidden_x, weight, metas, wfull, sendbuf, sendbuf_x, rows, stats, statrep, comb, statown,
    norms, tsums, e_all, g_all, gh_acc, ghsend, ghrecv, gw_ref,
    s_loc, s_hx, r_hx, s_meta, r_meta, s_w, r_w, s_row, r_row, s_rowx, r_rowx, s_fc, r_fc, s_fr, r_fr,
    s_sr, r_sr, s_so, r_so, s_gx, r_gx, s_gc, r_gc, s_gr, r_gr, s_gh, r_gh,
):
    labels, part = weight_hbm.shape
    samples = hidden_hbm.shape[0]
    cols = labels // 4
    o = lax.axis_index("own")
    r = lax.axis_index("rep")
    p1 = r + 1 - 2 * lax.rem(r, 2)
    p2 = lax.rem(r + 2, 4)
    p3 = lax.rem(p1 + 2, 4)
    row_count = n * depth
    pending = []
    local = [
        pltpu.make_async_copy(meta_hbm, meta, s_loc.at[0]),
        pltpu.make_async_copy(hidden_hbm, hidden, s_loc.at[1]),
        pltpu.make_async_copy(weight_hbm, weight, s_loc.at[2]),
        pltpu.make_async_copy(
            weight_hbm.at[pl.ds(pl.multiple_of(r * cols, cols), cols)],
            wfull.at[:, pl.ds(pl.multiple_of(r * part, part), part)],
            s_loc.at[3],
        ),
    ]

    def send(src, dst, ssem, rsem, own, rep):
        copy = pltpu.make_async_remote_copy(
            src_ref=src, dst_ref=dst, send_sem=ssem, recv_sem=rsem,
            device_id={"own": own, "rep": rep}, device_id_type=MESH,
        )
        copy.start()
        pending.append(copy)
        return copy

    def at_rows(s):
        return pl.ds(pl.multiple_of(s * depth, depth), depth)

    def at_part(q):
        return pl.ds(pl.multiple_of(q * part, part), part)

    def at_cols(q, c=0, size=None):
        size = cols if size is None else size
        return pl.ds(pl.multiple_of(q * cols + c * size, size), size)

    barrier = pltpu.get_barrier_semaphore()
    for k in range(1, n):
        pl.semaphore_signal(barrier, inc=1, device_id={"own": lax.rem(o + k, n), "rep": r}, device_id_type=MESH)
    for q in (p1, p2, p3):
        pl.semaphore_signal(barrier, inc=1, device_id={"own": o, "rep": q}, device_id_type=MESH)
    for c in local:
        c.start()
    local[0].wait()
    local[1].wait()
    below = lax.broadcasted_iota(jnp.int32, (samples, samples), 0)
    right = lax.broadcasted_iota(jnp.int32, (samples, samples), 1)
    upper = jnp.where(below < right, 1.0, 0.0).astype(BF16)

    def slots(ids):
        table = jnp.broadcast_to(meta[3:4, :], (n, samples))
        return lane_pick(table, jnp.broadcast_to(ids, (n, samples)))[: ids.shape[0]]

    mine = meta[...]
    own_rank = ranks(slots(mine[0:1]), slots(mine[1:2]), n, upper)
    place = lax.broadcasted_iota(jnp.int32, (depth, samples), 0)
    pack = jnp.concatenate(
        [jnp.where(own_rank[b : b + 1] == place, 1.0, 0.0).astype(BF16) for b in range(n)], axis=0
    )
    packed = jnp.dot(pack, hidden[...], preferred_element_type=F32).astype(BF16)
    for b in range(n):
        sendbuf[b] = packed[b * depth : (b + 1) * depth]
    pl.semaphore_wait(barrier, n - 1 + 3)
    hx = send(hidden_hbm, hidden_x, s_hx, r_hx, o, p2)
    row_copies = [
        send(sendbuf.at[lax.rem(o + k, n)], rows.at[at_rows(o), at_part(r)], s_row.at[k - 1], r_row.at[k - 1], lax.rem(o + k, n), r)
        for k in range(1, n)
    ]

    w_copies = [
        send(weight_hbm.at[at_cols(q)], wfull.at[:, at_part(r)], s_w.at[i], r_w.at[i], o, q)
        for i, q in ((1, p2), (2, p3), (0, p1))
    ]
    meta_copies = [
        send(meta_hbm, metas.at[o], s_meta.at[k - 1], r_meta.at[k - 1], lax.rem(o + k, n), r)
        for k in range(1, n)
    ]

    rows[at_rows(o), at_part(r)] = sendbuf[o]
    metas[o] = mine

    hx.wait_recv()
    packed_x = jnp.dot(pack, hidden_x[...], preferred_element_type=F32).astype(BF16)
    for b in range(n):
        sendbuf_x[b] = packed_x[b * depth : (b + 1) * depth]
    rowx_copies = [
        send(sendbuf_x.at[lax.rem(o + k, n)], rows.at[at_rows(o), at_part(p2)], s_rowx.at[k - 1], r_rowx.at[k - 1], lax.rem(o + k, n), r)
        for k in range(1, n)
    ]
    rows[at_rows(o), at_part(p2)] = sendbuf_x[o]

    fc, fr = [], []
    for k in range(n):
        s = lax.rem(o - k + n, n)
        if k > 0:
            row_copies[k - 1].wait_recv()
        block = rows.at[at_rows(s), at_part(r)]
        fc.append(send(block, block, s_fc.at[k], r_fc.at[k], o, p1))

    for c in meta_copies:
        c.wait_recv()
    slot0 = slots(metas[:, 0, :])
    slot1 = slots(metas[:, 1, :])
    pick = metas[:, 2, :]
    rank_all = ranks(slot0, slot1, n, upper)
    wanted = jnp.where(pick < labels, slot0, slot1)
    code = jnp.where(wanted == o, jnp.where(pick < labels, pick, pick - labels) + 1, 0)
    code_hi = (code // 64).astype(F32)
    code_lo = (code - (code // 64) * 64).astype(F32)
    lane = lax.broadcasted_iota(jnp.int32, (1, samples), 1)
    sub = lax.broadcasted_iota(jnp.int32, (8, samples), 0)
    bucket_sub = lax.broadcasted_iota(jnp.int32, (n, samples), 0)
    infos = []
    place2 = lax.broadcasted_iota(jnp.int32, (2 * depth, samples), 0)
    for sp in range(n // 2):
        info = jnp.zeros((8, 2 * depth), F32)
        for h in range(2):
            s = 2 * sp + h
            rank_me = jnp.max(
                jnp.where(bucket_sub == o, rank_all[s * n : (s + 1) * n], -1), axis=0, keepdims=True
            )
            member = jnp.where(
                (rank_me >= 0) & (rank_me + h * depth == place2), 1.0, 0.0
            ).astype(BF16)
            facts = jnp.where(
                sub == 0, lane.astype(F32),
                jnp.where(sub == 1, code_hi[s : s + 1], jnp.where(sub == 2, code_lo[s : s + 1], jnp.where(sub == 3, 1.0, 0.0))),
            ).astype(BF16)
            info = info + lax.dot_general(facts, member, NT, preferred_element_type=F32)
        infos.append(info)
    row_index = [x[0:1].astype(jnp.int32) for x in infos]
    row_valid = jnp.concatenate([x[3:4] for x in infos], axis=1) > 0.5
    row_target = jnp.concatenate([(x[1:2] * 64.0 + x[2:3]) for x in infos], axis=1).astype(jnp.int32) - 1

    for k in range(n):
        s = lax.rem(o - k + n, n)
        if k > 0:
            rowx_copies[k - 1].wait_recv()
        block = rows.at[at_rows(s), at_part(p2)]
        fr.append(send(block, block, s_fr.at[k], r_fr.at[k], o, p1))
    for k in range(n):
        fc[k].wait_recv()
    for c in w_copies:
        c.wait_recv()
    for k in range(n):
        fr[k].wait_recv()
    local[2].wait()
    local[3].wait()

    logits = lax.dot_general(wfull[...], rows[...], NT, preferred_element_type=F32)
    top = jnp.max(logits, axis=0, keepdims=True)
    label_id = lax.broadcasted_iota(jnp.int32, (cols, row_count), 0) + r * cols
    hot = label_id == row_target
    target_sum = jnp.sum(jnp.where(hot, logits, 0.0), axis=0, keepdims=True)
    raised = jnp.exp(logits - top)
    e_all[at_cols(r), :] = raised.astype(BF16)
    chunk = cols // 4
    gx, gc, gr = [], [], []
    for c in range(4):
        block = e_all.at[at_cols(r, c, chunk)]
        gx.append(send(block, block, s_gx.at[c], r_gx.at[c], o, p2))
        gc.append(send(block, block, s_gc.at[c], r_gc.at[c], o, p1))
    lse = top + jnp.log(jnp.sum(raised, axis=0, keepdims=True))
    for sp in range(n // 2):
        stats[sp : sp + 1, :] = lse[:, sp * 128 : (sp + 1) * 128]
        stats[n // 2 + sp : n // 2 + sp + 1, :] = target_sum[:, sp * 128 : (sp + 1) * 128]
        stats[n + sp : n + sp + 1, :] = top[:, sp * 128 : (sp + 1) * 128]
    stats[n + n // 2 :, :] = jnp.zeros((n // 2, samples), F32)
    sr = [
        send(stats, statrep.at[r], s_sr.at[i], r_sr.at[i], o, q)
        for i, q in ((1, p2), (2, p3), (0, p1))
    ]
    statrep[r] = stats[...]
    for c in sr:
        c.wait_recv()
    parts = [statrep[q, 0:n, :] for q in range(4)]
    high = jnp.maximum(jnp.maximum(parts[0], parts[1]), jnp.maximum(parts[2], parts[3]))
    total = high + jnp.log(sum(jnp.exp(x - high) for x in parts))
    is_lse = lax.broadcasted_iota(jnp.int32, (n, samples), 0) < n // 2
    comb[...] = jnp.where(is_lse, total, sum(parts))
    so = [
        send(comb, statown.at[o], s_so.at[k - 1], r_so.at[k - 1], lax.rem(o + k, n), r)
        for k in range(1, n)
    ]
    statown[o] = comb[...]
    for c in so:
        c.wait_recv()
    norm_rows = []
    for sp in range(n // 2):
        held = statown[:, sp, :]
        pair = []
        for h in range(2):
            s = 2 * sp + h
            rank = rank_all[s * n : (s + 1) * n]
            index = jnp.where(rank >= 0, rank + h * depth, 0)
            value = jnp.where(rank >= 0, lane_pick(held, index), -3.0e38)
            most = jnp.max(value, axis=0, keepdims=True)
            norm = most + jnp.log(jnp.sum(jnp.exp(value - most), axis=0, keepdims=True))
            norms[s : s + 1, :] = norm
            pair.append(
                lane_pick(jnp.broadcast_to(norm, (8, samples)), jnp.broadcast_to(row_index[sp], (8, samples)))[0:1]
            )
        norm_rows.append(jnp.where(lane < depth, pair[0], pair[1]))
    row_norm = jnp.concatenate(norm_rows, axis=1)

    def gradient(q, c, size):
        at = at_cols(q, c, size)
        tops = jnp.concatenate(
            [statrep[pl.ds(q, 1), n + sp : n + sp + 1, :].reshape(1, samples) for sp in range(n // 2)], axis=1
        )
        scale = jnp.where(row_valid, jnp.exp(tops - row_norm), 0.0)
        ids = lax.broadcasted_iota(jnp.int32, (size, row_count), 0) + (q * cols + c * size)
        grad = e_all[at, :].astype(F32) * scale - jnp.where(ids == row_target, 1.0, 0.0)
        g_all[at, :] = grad.astype(BF16)

    def row_term(q, c, size):
        at = at_cols(q, c, size)
        gradient(q, c, size)
        return lax.dot_general(g_all[at, :], weight[at, :], TN, preferred_element_type=F32)

    def weight_term(q, i):
        gw_ref[at_cols(q), :] = jnp.dot(
            g_all[at_cols(q), :], rows[:, at_part(r)], preferred_element_type=F32
        ).astype(BF16)
        out = pltpu.make_async_copy(gw_ref.at[at_cols(q)], gw_hbm.at[at_cols(q)], s_loc.at[4 + i])
        out.start()
        outs.append(out)

    outs = []
    gh_acc[...] = row_term(r, 0, cols)
    for c in range(4):
        gc[c].wait_recv()
    gh_acc[...] += row_term(p1, 0, cols)

    for sp in range(n // 2):
        held = statown[:, n // 2 + sp, :]
        for h in range(2):
            s = 2 * sp + h
            rank = rank_all[s * n : (s + 1) * n]
            index = jnp.where(rank >= 0, rank + h * depth, 0)
            value = jnp.where(rank >= 0, lane_pick(held, index), 0.0)
            tsums[s : s + 1, :] = jnp.sum(value, axis=0, keepdims=True)
    loss_ref[...] = norms[pl.ds(o, 1), :] - tsums[pl.ds(o, 1), :]

    weight_term(r, 0)
    weight_term(p1, 1)
    for c in range(4):
        gx[c].wait_recv()
        block = e_all.at[at_cols(p2, c, chunk)]
        gr.append(send(block, block, s_gr.at[c], r_gr.at[c], o, p1))
        gh_acc[...] += row_term(p2, c, chunk)
    for c in range(4):
        gr[c].wait_recv()
    ghsend[...] = (gh_acc[...] + row_term(p3, 0, cols)).astype(BF16)
    back = [
        send(ghsend.at[at_rows(lax.rem(o + k, n))], ghrecv.at[at_rows(o)], s_gh.at[k - 1], r_gh.at[k - 1], lax.rem(o + k, n), r)
        for k in range(1, n)
    ]
    ghrecv[at_rows(o), :] = ghsend[at_rows(o), :]
    weight_term(p2, 2)
    weight_term(p3, 3)
    for c in back:
        c.wait_recv()
    gh_ref[...] = lax.dot_general(pack, ghrecv[...], TN, preferred_element_type=F32)
    for c in pending:
        c.wait_send()
    for c in outs:
        c.wait()


def fused(hidden, weight, bucket_map, active, label_pick):
    samples, part = hidden.shape
    labels = weight.shape[1]
    n = bucket_map.shape[0]
    depth = 2 * samples * active.shape[1] // n
    cols = labels // 4
    row_count = n * depth
    meta = jnp.concatenate(
        [
            active.T,
            label_pick[None],
            jnp.pad(bucket_map, (0, samples - n))[None],
            jnp.zeros((4, samples), jnp.int32),
        ],
        axis=0,
    )
    vmem = pl.BlockSpec(memory_space=pltpu.VMEM)
    dma = pltpu.SemaphoreType.DMA
    sems = [dma((8,)), dma, dma]
    for count in (n - 1, 3, n - 1, n - 1, n, n, 3, n - 1, 4, 4, 4, n - 1):
        sems += [dma((count,)), dma((count,))]
    anyspace = pl.BlockSpec(memory_space=pl.ANY)
    loss, grad_hidden, grad_weight = pl.pallas_call(
        functools.partial(kernel, n, depth),
        out_shape=(
            jax.ShapeDtypeStruct((1, samples), F32),
            jax.ShapeDtypeStruct((samples, part), F32),
            jax.ShapeDtypeStruct((labels, part), BF16),
        ),
        in_specs=[anyspace, anyspace, anyspace],
        out_specs=(vmem, vmem, anyspace),
        scratch_shapes=[
            pltpu.VMEM((8, samples), jnp.int32),
            pltpu.VMEM((samples, part), BF16),
            pltpu.VMEM((samples, part), BF16),
            pltpu.VMEM((labels, part), BF16),
            pltpu.VMEM((n, 8, samples), jnp.int32),
            pltpu.VMEM((cols, 4 * part), BF16),
            pltpu.VMEM((n, depth, part), BF16),
            pltpu.VMEM((n, depth, part), BF16),
            pltpu.VMEM((row_count, 4 * part), BF16),
            pltpu.VMEM((2 * n, samples), F32),
            pltpu.VMEM((4, 2 * n, samples), F32),
            pltpu.VMEM((n, samples), F32),
            pltpu.VMEM((n, n, samples), F32),
            pltpu.VMEM((n, samples), F32),
            pltpu.VMEM((n, samples), F32),
            pltpu.VMEM((labels, row_count), BF16),
            pltpu.VMEM((labels, row_count), BF16),
            pltpu.VMEM((row_count, part), F32),
            pltpu.VMEM((row_count, part), BF16),
            pltpu.VMEM((row_count, part), BF16),
            pltpu.VMEM((labels, part), BF16),
        ] + sems,
        compiler_params=pltpu.CompilerParams(
            collective_id=0, has_side_effects=True, vmem_limit_bytes=48 * 1024 * 1024
        ),
    )(meta, hidden, weight[0])
    return loss[0], grad_hidden, grad_weight[None]


def body(hidden, weight, bucket_map, active, label_pick):
    samp_count = hidden.shape[0]
    bucket_dev, label_count, feature_part = weight.shape
    picks = active.shape[1]
    bucket_total = bucket_map.shape[0]
    owner_count = lax.axis_size("own")
    slot_depth = max(2, 2 * samp_count * picks // bucket_total)
    pair_count = samp_count * picks
    slots_total = bucket_total * slot_depth
    row_count = owner_count * slot_depth
    pair_bucket = active.reshape(pair_count)
    bucket_iota = lax.broadcasted_iota(jnp.int32, (pair_count, bucket_total), 1)
    slot_index = jnp.sum(
        jnp.where(pair_bucket[:, None] == bucket_iota, bucket_map[None, :], 0), axis=1
    )
    slot_hits = (slot_index[:, None] == bucket_iota).astype(jnp.int32)
    earlier = jnp.cumsum(slot_hits, axis=0) - slot_hits
    rank_within = jnp.sum(earlier * slot_hits, axis=1)
    position = slot_index * slot_depth + rank_within
    pair_index = jnp.arange(pair_count, dtype=jnp.int32)
    pick_value = jnp.repeat(label_pick, picks)
    target_pair = jnp.where(
        pick_value // label_count == pair_index % picks, pick_value % label_count, -1
    )
    width_sent = hidden.shape[1]
    pair_rows = jnp.repeat(hidden, picks, axis=0)
    send_rows = jnp.zeros((slots_total, width_sent), jnp.bfloat16).at[position].set(pair_rows)
    send_target = jnp.full((slots_total,), -1, jnp.int32).at[position].set(target_pair)
    got_rows, got_target = (
        lax.all_to_all(
            send_rows.reshape(owner_count, bucket_dev * slot_depth, width_sent),
            "own",
            split_axis=0,
            concat_axis=0,
            tiled=True,
        ),
        lax.all_to_all(
            send_target.reshape(owner_count, bucket_dev * slot_depth),
            "own",
            split_axis=0,
            concat_axis=0,
            tiled=True,
        ),
    )
    received = got_rows.reshape(owner_count, bucket_dev, slot_depth, width_sent).transpose(
        1, 0, 2, 3
    )
    received = received.reshape(bucket_dev, row_count, width_sent)
    target_col = (
        got_target.reshape(owner_count, bucket_dev, slot_depth)
        .transpose(1, 0, 2)
        .reshape(bucket_dev, row_count)
    )
    partial_value = jnp.einsum("brd,bcd->brc", received, weight, preferred_element_type=jnp.float32)
    logits = lax.psum(partial_value, "rep")
    columns = lax.broadcasted_iota(jnp.int32, (1, 1, label_count), 2)
    row_max = jnp.max(logits, axis=2)
    row_sum = jnp.sum(jnp.exp(logits - row_max[..., None]), axis=2)
    row_target = jnp.sum(jnp.where(columns == target_col[..., None], logits, 0.0), axis=2)

    def to_sources(values):
        return (
            values.reshape(bucket_dev, owner_count, slot_depth)
            .transpose(1, 0, 2)
            .reshape(owner_count, bucket_dev * slot_depth)
        )

    back_max, back_sum, back_target = (
        lax.all_to_all(to_sources(row_max), "own", split_axis=0, concat_axis=0, tiled=True),
        lax.all_to_all(to_sources(row_sum), "own", split_axis=0, concat_axis=0, tiled=True),
        lax.all_to_all(to_sources(row_target), "own", split_axis=0, concat_axis=0, tiled=True),
    )
    pair_max = back_max.reshape(slots_total)[position].reshape(samp_count, picks)
    pair_sum = back_sum.reshape(slots_total)[position].reshape(samp_count, picks)
    pair_target = back_target.reshape(slots_total)[position].reshape(samp_count, picks)
    peak_max = jnp.max(pair_max, axis=1)
    norm_sum = jnp.sum(pair_sum * jnp.exp(pair_max - peak_max[:, None]), axis=1)
    log_norm = peak_max + jnp.log(norm_sum)
    sample_loss = log_norm - jnp.sum(pair_target, axis=1)
    send_norm = jnp.zeros((slots_total,), jnp.float32).at[position].set(jnp.repeat(log_norm, picks))
    got_norm = lax.all_to_all(
        send_norm.reshape(owner_count, bucket_dev * slot_depth),
        "own",
        split_axis=0,
        concat_axis=0,
        tiled=True,
    )
    row_norm = (
        got_norm.reshape(owner_count, bucket_dev, slot_depth)
        .transpose(1, 0, 2)
        .reshape(bucket_dev, row_count)
    )
    onehot = (columns == target_col[..., None]).astype(jnp.float32)
    grad_logits = (jnp.exp(logits - row_norm[..., None]) - onehot).astype(jnp.bfloat16)
    grad_weight = jnp.einsum(
        "brc,brd->bcd", grad_logits, received, preferred_element_type=jnp.float32
    ).astype(jnp.bfloat16)
    row_grads = jnp.einsum("brc,bcd->brd", grad_logits, weight, preferred_element_type=jnp.float32)
    send_grads = row_grads.reshape(bucket_dev, owner_count, slot_depth, feature_part).transpose(
        1, 0, 2, 3
    )
    send_grads = send_grads.reshape(owner_count, bucket_dev * slot_depth, feature_part)
    got_grads = lax.all_to_all(send_grads, "own", split_axis=0, concat_axis=0, tiled=True)
    pair_grads = got_grads.reshape(slots_total, feature_part)[position].reshape(
        samp_count, picks, feature_part
    )
    grad_hidden = jnp.sum(pair_grads, axis=1)
    return (sample_loss, grad_hidden, grad_weight)


def choose(hidden, weight, bucket_map, active, label_pick):
    samples, picks = active.shape
    buckets = bucket_map.shape[0]
    depth = 2 * samples * picks // buckets
    fits = (
        weight.shape[0] == 1
        and lax.axis_size("rep") == 4
        and buckets == 8
        and picks == 2
        and samples == 128
        and 2 * depth == samples
        and weight.shape[1] % 512 == 0
        and hidden.shape[1] % 128 == 0
    )
    run = fused if fits else body
    return run(hidden, weight, bucket_map, active, label_pick)


def solution(mesh):
    in_specs = (P("own", "rep"), P("own", None, "rep"), P(), P("own", None), P("own"))
    out_specs = (P("own"), P("own", "rep"), P("own", None, "rep"))
    return jax.shard_map(choose, mesh=mesh, in_specs=in_specs, out_specs=out_specs, check_vma=False)
```

```python
import functools
import jax
import jax.numpy as jnp
from jax import lax
from jax.experimental import pallas as pl
from jax.experimental.pallas import tpu as pltpu
from jax.sharding import PartitionSpec as P

MESH = pl.DeviceIdType.MESH
F32 = jnp.float32
BF16 = jnp.bfloat16
NT = (((1,), (1,)), ((), ()))
TN = (((0,), (0,)), ((), ()))


def ranks(slot0, slot1, buckets, upper):
    sources, samples = slot0.shape
    bucket = lax.broadcasted_iota(jnp.int32, (buckets, samples), 0)
    hits = [
        jnp.where((slot0[s : s + 1] == bucket) | (slot1[s : s + 1] == bucket), 1.0, 0.0)
        for s in range(sources)
    ]
    hits = jnp.concatenate(hits, axis=0) if sources > 1 else hits[0]
    earlier = jnp.dot(hits.astype(BF16), upper, preferred_element_type=F32)
    return jnp.where(hits > 0.5, earlier, -1.0).astype(jnp.int32)


def lane_pick(values, index):
    return jnp.take_along_axis(values, index, axis=1)


def kernel(
    n, depth, act_hbm, pick_hbm, map_hbm, hidden_hbm, weight_hbm,
    loss_ref, gh_ref, gw_hbm,
    act, pick_own, table_in, meta, hidden, hidden_x, weight, metas, wfull, sendbuf, sendbuf_x, rows, stats, statrep, comb, statown,
    norms, tsums, e_all, g_all, gh_acc, ghsend, ghrecv, gw_ref,
    s_loc, s_hx, r_hx, s_meta, r_meta, s_w, r_w, s_row, r_row, s_rowx, r_rowx, s_fc, r_fc, s_fr, r_fr,
    s_sr, r_sr, s_so, r_so, s_gx, r_gx, s_gc, r_gc, s_gr, r_gr, s_gh, r_gh,
):
    labels, part = weight_hbm.shape
    samples = hidden_hbm.shape[0]
    cols = labels // 4
    o = lax.axis_index("own")
    r = lax.axis_index("rep")
    p1 = r + 1 - 2 * lax.rem(r, 2)
    p2 = lax.rem(r + 2, 4)
    p3 = lax.rem(p1 + 2, 4)
    row_count = n * depth
    pending = []
    local = [
        pltpu.make_async_copy(act_hbm, act, s_loc.at[0]),
        pltpu.make_async_copy(hidden_hbm, hidden, s_loc.at[1]),
        pltpu.make_async_copy(weight_hbm, weight, s_loc.at[2]),
        pltpu.make_async_copy(
            weight_hbm.at[pl.ds(pl.multiple_of(r * cols, cols), cols)],
            wfull.at[:, pl.ds(pl.multiple_of(r * part, part), part)],
            s_loc.at[3],
        ),
        pltpu.make_async_copy(pick_hbm, pick_own, s_loc.at[8]),
        pltpu.make_async_copy(map_hbm, table_in, s_loc.at[9]),
    ]

    def send(src, dst, ssem, rsem, own, rep):
        copy = pltpu.make_async_remote_copy(
            src_ref=src, dst_ref=dst, send_sem=ssem, recv_sem=rsem,
            device_id={"own": own, "rep": rep}, device_id_type=MESH,
        )
        copy.start()
        pending.append(copy)
        return copy

    def at_rows(s):
        return pl.ds(pl.multiple_of(s * depth, depth), depth)

    def at_part(q):
        return pl.ds(pl.multiple_of(q * part, part), part)

    def at_cols(q, c=0, size=None):
        size = cols if size is None else size
        return pl.ds(pl.multiple_of(q * cols + c * size, size), size)

    barrier = pltpu.get_barrier_semaphore()
    for k in range(1, n):
        pl.semaphore_signal(barrier, inc=1, device_id={"own": lax.rem(o + k, n), "rep": r}, device_id_type=MESH)
    for q in (p1, p2, p3):
        pl.semaphore_signal(barrier, inc=1, device_id={"own": o, "rep": q}, device_id_type=MESH)
    for c in local:
        c.start()
    local[0].wait()
    local[4].wait()
    local[5].wait()
    meta[0:2, :] = act[...]
    meta[2:3, :] = pick_own[...]
    meta[3:8, :] = jnp.zeros((5, samples), jnp.int32)
    meta[3:4, 0:n] = table_in[...]
    local[1].wait()
    below = lax.broadcasted_iota(jnp.int32, (samples, samples), 0)
    right = lax.broadcasted_iota(jnp.int32, (samples, samples), 1)
    upper = jnp.where(below < right, 1.0, 0.0).astype(BF16)

    def slots(ids):
        table = jnp.broadcast_to(meta[3:4, :], (n, samples))
        return lane_pick(table, jnp.broadcast_to(ids, (n, samples)))[: ids.shape[0]]

    mine = meta[...]
    own_rank = ranks(slots(mine[0:1]), slots(mine[1:2]), n, upper)
    place = lax.broadcasted_iota(jnp.int32, (depth, samples), 0)
    pack = jnp.concatenate(
        [jnp.where(own_rank[b : b + 1] == place, 1.0, 0.0).astype(BF16) for b in range(n)], axis=0
    )
    packed = jnp.dot(pack, hidden[...], preferred_element_type=F32).astype(BF16)
    for b in range(n):
        sendbuf[b] = packed[b * depth : (b + 1) * depth]
    pl.semaphore_wait(barrier, n - 1 + 3)
    hx = send(hidden_hbm, hidden_x, s_hx, r_hx, o, p2)
    row_copies = [
        send(sendbuf.at[lax.rem(o + k, n)], rows.at[at_rows(o), at_part(r)], s_row.at[k - 1], r_row.at[k - 1], lax.rem(o + k, n), r)
        for k in range(1, n)
    ]

    w_copies = [
        send(weight_hbm.at[at_cols(q)], wfull.at[:, at_part(r)], s_w.at[i], r_w.at[i], o, q)
        for i, q in ((1, p2), (2, p3), (0, p1))
    ]
    meta_copies = [
        send(meta, metas.at[o], s_meta.at[k - 1], r_meta.at[k - 1], lax.rem(o + k, n), r)
        for k in range(1, n)
    ]

    rows[at_rows(o), at_part(r)] = sendbuf[o]
    metas[o] = mine

    hx.wait_recv()
    packed_x = jnp.dot(pack, hidden_x[...], preferred_element_type=F32).astype(BF16)
    for b in range(n):
        sendbuf_x[b] = packed_x[b * depth : (b + 1) * depth]
    rowx_copies = [
        send(sendbuf_x.at[lax.rem(o + k, n)], rows.at[at_rows(o), at_part(p2)], s_rowx.at[k - 1], r_rowx.at[k - 1], lax.rem(o + k, n), r)
        for k in range(1, n)
    ]
    rows[at_rows(o), at_part(p2)] = sendbuf_x[o]

    fc, fr = [], []
    for k in range(n):
        s = lax.rem(o - k + n, n)
        if k > 0:
            row_copies[k - 1].wait_recv()
        block = rows.at[at_rows(s), at_part(r)]
        fc.append(send(block, block, s_fc.at[k], r_fc.at[k], o, p1))

    for c in meta_copies:
        c.wait_recv()
    slot0 = slots(metas[:, 0, :])
    slot1 = slots(metas[:, 1, :])
    pick = metas[:, 2, :]
    rank_all = ranks(slot0, slot1, n, upper)
    wanted = jnp.where(pick < labels, slot0, slot1)
    code = jnp.where(wanted == o, jnp.where(pick < labels, pick, pick - labels) + 1, 0)
    code_hi = (code // 64).astype(F32)
    code_lo = (code - (code // 64) * 64).astype(F32)
    lane = lax.broadcasted_iota(jnp.int32, (1, samples), 1)
    sub = lax.broadcasted_iota(jnp.int32, (8, samples), 0)
    bucket_sub = lax.broadcasted_iota(jnp.int32, (n, samples), 0)
    infos = []
    place2 = lax.broadcasted_iota(jnp.int32, (2 * depth, samples), 0)
    for sp in range(n // 2):
        info = jnp.zeros((8, 2 * depth), F32)
        for h in range(2):
            s = 2 * sp + h
            rank_me = jnp.max(
                jnp.where(bucket_sub == o, rank_all[s * n : (s + 1) * n], -1), axis=0, keepdims=True
            )
            member = jnp.where(
                (rank_me >= 0) & (rank_me + h * depth == place2), 1.0, 0.0
            ).astype(BF16)
            facts = jnp.where(
                sub == 0, lane.astype(F32),
                jnp.where(sub == 1, code_hi[s : s + 1], jnp.where(sub == 2, code_lo[s : s + 1], jnp.where(sub == 3, 1.0, 0.0))),
            ).astype(BF16)
            info = info + lax.dot_general(facts, member, NT, preferred_element_type=F32)
        infos.append(info)
    row_index = [x[0:1].astype(jnp.int32) for x in infos]
    row_valid = jnp.concatenate([x[3:4] for x in infos], axis=1) > 0.5
    row_target = jnp.concatenate([(x[1:2] * 64.0 + x[2:3]) for x in infos], axis=1).astype(jnp.int32) - 1

    for k in range(n):
        s = lax.rem(o - k + n, n)
        if k > 0:
            rowx_copies[k - 1].wait_recv()
        block = rows.at[at_rows(s), at_part(p2)]
        fr.append(send(block, block, s_fr.at[k], r_fr.at[k], o, p1))
    for k in range(n):
        fc[k].wait_recv()
    for c in w_copies:
        c.wait_recv()
    for k in range(n):
        fr[k].wait_recv()
    local[2].wait()
    local[3].wait()

    logits = lax.dot_general(wfull[...], rows[...], NT, preferred_element_type=F32)
    top = jnp.max(logits, axis=0, keepdims=True)
    label_id = lax.broadcasted_iota(jnp.int32, (cols, row_count), 0) + r * cols
    hot = label_id == row_target
    target_sum = jnp.sum(jnp.where(hot, logits, 0.0), axis=0, keepdims=True)
    raised = jnp.exp(logits - top)
    lse = top + jnp.log(jnp.sum(raised, axis=0, keepdims=True))
    for sp in range(n // 2):
        stats[sp : sp + 1, :] = lse[:, sp * 128 : (sp + 1) * 128]
        stats[n // 2 + sp : n // 2 + sp + 1, :] = target_sum[:, sp * 128 : (sp + 1) * 128]
        stats[n + sp : n + sp + 1, :] = top[:, sp * 128 : (sp + 1) * 128]
    stats[n + n // 2 :, :] = jnp.zeros((n // 2, samples), F32)
    sr = [
        send(stats, statrep.at[r], s_sr.at[i], r_sr.at[i], o, q)
        for i, q in ((1, p2), (2, p3), (0, p1))
    ]
    e_all[at_cols(r), :] = raised.astype(BF16)
    chunk = cols // 4
    gx, gc, gr = [], [], []
    for c in range(4):
        block = e_all.at[at_cols(r, c, chunk)]
        gx.append(send(block, block, s_gx.at[c], r_gx.at[c], o, p2))
        gc.append(send(block, block, s_gc.at[c], r_gc.at[c], o, p1))
    statrep[r] = stats[...]
    for c in sr:
        c.wait_recv()
    parts = [statrep[q, 0:n, :] for q in range(4)]
    high = jnp.maximum(jnp.maximum(parts[0], parts[1]), jnp.maximum(parts[2], parts[3]))
    total = high + jnp.log(sum(jnp.exp(x - high) for x in parts))
    is_lse = lax.broadcasted_iota(jnp.int32, (n, samples), 0) < n // 2
    comb[...] = jnp.where(is_lse, total, sum(parts))
    so = [
        send(comb, statown.at[o], s_so.at[k - 1], r_so.at[k - 1], lax.rem(o + k, n), r)
        for k in range(1, n)
    ]
    statown[o] = comb[...]
    for c in so:
        c.wait_recv()
    norm_rows = []
    for sp in range(n // 2):
        held = statown[:, sp, :]
        pair = []
        for h in range(2):
            s = 2 * sp + h
            rank = rank_all[s * n : (s + 1) * n]
            index = jnp.where(rank >= 0, rank + h * depth, 0)
            value = jnp.where(rank >= 0, lane_pick(held, index), -3.0e38)
            most = jnp.max(value, axis=0, keepdims=True)
            norm = most + jnp.log(jnp.sum(jnp.exp(value - most), axis=0, keepdims=True))
            norms[s : s + 1, :] = norm
            pair.append(
                lane_pick(jnp.broadcast_to(norm, (8, samples)), jnp.broadcast_to(row_index[sp], (8, samples)))[0:1]
            )
        norm_rows.append(jnp.where(lane < depth, pair[0], pair[1]))
    row_norm = jnp.concatenate(norm_rows, axis=1)

    def gradient(q, c, size):
        at = at_cols(q, c, size)
        tops = jnp.concatenate(
            [statrep[pl.ds(q, 1), n + sp : n + sp + 1, :].reshape(1, samples) for sp in range(n // 2)], axis=1
        )
        scale = jnp.where(row_valid, jnp.exp(tops - row_norm), 0.0)
        ids = lax.broadcasted_iota(jnp.int32, (size, row_count), 0) + (q * cols + c * size)
        grad = e_all[at, :].astype(F32) * scale - jnp.where(ids == row_target, 1.0, 0.0)
        g_all[at, :] = grad.astype(BF16)

    def row_term(q, c, size):
        at = at_cols(q, c, size)
        gradient(q, c, size)
        return lax.dot_general(g_all[at, :], weight[at, :], TN, preferred_element_type=F32)

    def weight_term(q, i):
        gw_ref[at_cols(q), :] = jnp.dot(
            g_all[at_cols(q), :], rows[:, at_part(r)], preferred_element_type=F32
        ).astype(BF16)
        out = pltpu.make_async_copy(gw_ref.at[at_cols(q)], gw_hbm.at[at_cols(q)], s_loc.at[4 + i])
        out.start()
        outs.append(out)

    outs = []
    gh_acc[...] = row_term(r, 0, cols)
    for c in range(4):
        gc[c].wait_recv()
    gh_acc[...] += row_term(p1, 0, cols)

    for sp in range(n // 2):
        held = statown[:, n // 2 + sp, :]
        for h in range(2):
            s = 2 * sp + h
            rank = rank_all[s * n : (s + 1) * n]
            index = jnp.where(rank >= 0, rank + h * depth, 0)
            value = jnp.where(rank >= 0, lane_pick(held, index), 0.0)
            tsums[s : s + 1, :] = jnp.sum(value, axis=0, keepdims=True)
    loss_ref[...] = norms[pl.ds(o, 1), :] - tsums[pl.ds(o, 1), :]

    weight_term(r, 0)
    weight_term(p1, 1)
    for c in range(4):
        gx[c].wait_recv()
        block = e_all.at[at_cols(p2, c, chunk)]
        gr.append(send(block, block, s_gr.at[c], r_gr.at[c], o, p1))
        gh_acc[...] += row_term(p2, c, chunk)
    for c in range(4):
        gr[c].wait_recv()
    ghsend[...] = (gh_acc[...] + row_term(p3, 0, cols)).astype(BF16)
    back = [
        send(ghsend.at[at_rows(lax.rem(o + k, n))], ghrecv.at[at_rows(o)], s_gh.at[k - 1], r_gh.at[k - 1], lax.rem(o + k, n), r)
        for k in range(1, n)
    ]
    ghrecv[at_rows(o), :] = ghsend[at_rows(o), :]
    weight_term(p2, 2)
    weight_term(p3, 3)
    for c in back:
        c.wait_recv()
    gh_ref[...] = lax.dot_general(pack, ghrecv[...], TN, preferred_element_type=F32)
    for c in pending:
        c.wait_send()
    for c in outs:
        c.wait()


def fused(hidden, weight, bucket_map, active, label_pick):
    samples, part = hidden.shape
    labels = weight.shape[1]
    n = bucket_map.shape[0]
    depth = 2 * samples * active.shape[1] // n
    cols = labels // 4
    row_count = n * depth
    vmem = pl.BlockSpec(memory_space=pltpu.VMEM)
    dma = pltpu.SemaphoreType.DMA
    sems = [dma((10,)), dma, dma]
    for count in (n - 1, 3, n - 1, n - 1, n, n, 3, n - 1, 4, 4, 4, n - 1):
        sems += [dma((count,)), dma((count,))]
    hbm = pl.BlockSpec(memory_space=pltpu.HBM)
    loss, grad_hidden, grad_weight = pl.pallas_call(
        functools.partial(kernel, n, depth),
        out_shape=(
            jax.ShapeDtypeStruct((1, samples), F32),
            jax.ShapeDtypeStruct((samples, part), F32),
            jax.ShapeDtypeStruct((labels, part), BF16),
        ),
        in_specs=[hbm] * 5,
        out_specs=(vmem, vmem, hbm),
        scratch_shapes=[
            pltpu.VMEM((2, samples), jnp.int32),
            pltpu.VMEM((1, samples), jnp.int32),
            pltpu.VMEM((1, n), jnp.int32),
            pltpu.VMEM((8, samples), jnp.int32),
            pltpu.VMEM((samples, part), BF16),
            pltpu.VMEM((samples, part), BF16),
            pltpu.VMEM((labels, part), BF16),
            pltpu.VMEM((n, 8, samples), jnp.int32),
            pltpu.VMEM((cols, 4 * part), BF16),
            pltpu.VMEM((n, depth, part), BF16),
            pltpu.VMEM((n, depth, part), BF16),
            pltpu.VMEM((row_count, 4 * part), BF16),
            pltpu.VMEM((2 * n, samples), F32),
            pltpu.VMEM((4, 2 * n, samples), F32),
            pltpu.VMEM((n, samples), F32),
            pltpu.VMEM((n, n, samples), F32),
            pltpu.VMEM((n, samples), F32),
            pltpu.VMEM((n, samples), F32),
            pltpu.VMEM((labels, row_count), BF16),
            pltpu.VMEM((labels, row_count), BF16),
            pltpu.VMEM((row_count, part), F32),
            pltpu.VMEM((row_count, part), BF16),
            pltpu.VMEM((row_count, part), BF16),
            pltpu.VMEM((labels, part), BF16),
        ] + sems,
        compiler_params=pltpu.CompilerParams(
            collective_id=0, has_side_effects=True, vmem_limit_bytes=60 * 1024 * 1024
        ),
    )(active.T, label_pick[None], bucket_map[None], hidden, weight[0])
    return loss[0], grad_hidden, grad_weight[None]


def body(hidden, weight, bucket_map, active, label_pick):
    samp_count = hidden.shape[0]
    bucket_dev, label_count, feature_part = weight.shape
    picks = active.shape[1]
    bucket_total = bucket_map.shape[0]
    owner_count = lax.axis_size("own")
    slot_depth = max(2, 2 * samp_count * picks // bucket_total)
    pair_count = samp_count * picks
    slots_total = bucket_total * slot_depth
    row_count = owner_count * slot_depth
    pair_bucket = active.reshape(pair_count)
    bucket_iota = lax.broadcasted_iota(jnp.int32, (pair_count, bucket_total), 1)
    slot_index = jnp.sum(
        jnp.where(pair_bucket[:, None] == bucket_iota, bucket_map[None, :], 0), axis=1
    )
    slot_hits = (slot_index[:, None] == bucket_iota).astype(jnp.int32)
    earlier = jnp.cumsum(slot_hits, axis=0) - slot_hits
    rank_within = jnp.sum(earlier * slot_hits, axis=1)
    position = slot_index * slot_depth + rank_within
    pair_index = jnp.arange(pair_count, dtype=jnp.int32)
    pick_value = jnp.repeat(label_pick, picks)
    target_pair = jnp.where(
        pick_value // label_count == pair_index % picks, pick_value % label_count, -1
    )
    width_sent = hidden.shape[1]
    pair_rows = jnp.repeat(hidden, picks, axis=0)
    send_rows = jnp.zeros((slots_total, width_sent), jnp.bfloat16).at[position].set(pair_rows)
    send_target = jnp.full((slots_total,), -1, jnp.int32).at[position].set(target_pair)
    got_rows, got_target = (
        lax.all_to_all(
            send_rows.reshape(owner_count, bucket_dev * slot_depth, width_sent),
            "own",
            split_axis=0,
            concat_axis=0,
            tiled=True,
        ),
        lax.all_to_all(
            send_target.reshape(owner_count, bucket_dev * slot_depth),
            "own",
            split_axis=0,
            concat_axis=0,
            tiled=True,
        ),
    )
    received = got_rows.reshape(owner_count, bucket_dev, slot_depth, width_sent).transpose(
        1, 0, 2, 3
    )
    received = received.reshape(bucket_dev, row_count, width_sent)
    target_col = (
        got_target.reshape(owner_count, bucket_dev, slot_depth)
        .transpose(1, 0, 2)
        .reshape(bucket_dev, row_count)
    )
    partial_value = jnp.einsum("brd,bcd->brc", received, weight, preferred_element_type=jnp.float32)
    logits = lax.psum(partial_value, "rep")
    columns = lax.broadcasted_iota(jnp.int32, (1, 1, label_count), 2)
    row_max = jnp.max(logits, axis=2)
    row_sum = jnp.sum(jnp.exp(logits - row_max[..., None]), axis=2)
    row_target = jnp.sum(jnp.where(columns == target_col[..., None], logits, 0.0), axis=2)

    def to_sources(values):
        return (
            values.reshape(bucket_dev, owner_count, slot_depth)
            .transpose(1, 0, 2)
            .reshape(owner_count, bucket_dev * slot_depth)
        )

    back_max, back_sum, back_target = (
        lax.all_to_all(to_sources(row_max), "own", split_axis=0, concat_axis=0, tiled=True),
        lax.all_to_all(to_sources(row_sum), "own", split_axis=0, concat_axis=0, tiled=True),
        lax.all_to_all(to_sources(row_target), "own", split_axis=0, concat_axis=0, tiled=True),
    )
    pair_max = back_max.reshape(slots_total)[position].reshape(samp_count, picks)
    pair_sum = back_sum.reshape(slots_total)[position].reshape(samp_count, picks)
    pair_target = back_target.reshape(slots_total)[position].reshape(samp_count, picks)
    peak_max = jnp.max(pair_max, axis=1)
    norm_sum = jnp.sum(pair_sum * jnp.exp(pair_max - peak_max[:, None]), axis=1)
    log_norm = peak_max + jnp.log(norm_sum)
    sample_loss = log_norm - jnp.sum(pair_target, axis=1)
    send_norm = jnp.zeros((slots_total,), jnp.float32).at[position].set(jnp.repeat(log_norm, picks))
    got_norm = lax.all_to_all(
        send_norm.reshape(owner_count, bucket_dev * slot_depth),
        "own",
        split_axis=0,
        concat_axis=0,
        tiled=True,
    )
    row_norm = (
        got_norm.reshape(owner_count, bucket_dev, slot_depth)
        .transpose(1, 0, 2)
        .reshape(bucket_dev, row_count)
    )
    onehot = (columns == target_col[..., None]).astype(jnp.float32)
    grad_logits = (jnp.exp(logits - row_norm[..., None]) - onehot).astype(jnp.bfloat16)
    grad_weight = jnp.einsum(
        "brc,brd->bcd", grad_logits, received, preferred_element_type=jnp.float32
    ).astype(jnp.bfloat16)
    row_grads = jnp.einsum("brc,bcd->brd", grad_logits, weight, preferred_element_type=jnp.float32)
    send_grads = row_grads.reshape(bucket_dev, owner_count, slot_depth, feature_part).transpose(
        1, 0, 2, 3
    )
    send_grads = send_grads.reshape(owner_count, bucket_dev * slot_depth, feature_part)
    got_grads = lax.all_to_all(send_grads, "own", split_axis=0, concat_axis=0, tiled=True)
    pair_grads = got_grads.reshape(slots_total, feature_part)[position].reshape(
        samp_count, picks, feature_part
    )
    grad_hidden = jnp.sum(pair_grads, axis=1)
    return (sample_loss, grad_hidden, grad_weight)


def choose(hidden, weight, bucket_map, active, label_pick):
    samples, picks = active.shape
    buckets = bucket_map.shape[0]
    depth = 2 * samples * picks // buckets
    fits = (
        weight.shape[0] == 1
        and lax.axis_size("rep") == 4
        and buckets == 8
        and picks == 2
        and samples == 128
        and 2 * depth == samples
        and weight.shape[1] % 512 == 0
        and hidden.shape[1] % 128 == 0
    )
    run = fused if fits else body
    return run(hidden, weight, bucket_map, active, label_pick)


def solution(mesh):
    in_specs = (P("own", "rep"), P("own", None, "rep"), P(), P("own", None), P("own"))
    out_specs = (P("own"), P("own", "rep"), P("own", None, "rep"))
    return jax.shard_map(choose, mesh=mesh, in_specs=in_specs, out_specs=out_specs, check_vma=False)
```

```python
import functools
import jax
import jax.numpy as jnp
from jax import lax
from jax.experimental import pallas as pl
from jax.experimental.pallas import tpu as pltpu
from jax.sharding import PartitionSpec as P

MESH = pl.DeviceIdType.MESH
F32 = jnp.float32
BF16 = jnp.bfloat16
NT = (((1,), (1,)), ((), ()))
TN = (((0,), (0,)), ((), ()))


def ranks(slot0, slot1, buckets, upper):
    sources, samples = slot0.shape
    bucket = lax.broadcasted_iota(jnp.int32, (buckets, samples), 0)
    hits = [
        jnp.where((slot0[s : s + 1] == bucket) | (slot1[s : s + 1] == bucket), 1.0, 0.0)
        for s in range(sources)
    ]
    hits = jnp.concatenate(hits, axis=0) if sources > 1 else hits[0]
    earlier = jnp.dot(hits.astype(BF16), upper, preferred_element_type=F32)
    return jnp.where(hits > 0.5, earlier, -1.0).astype(jnp.int32)


def lane_pick(values, index):
    return jnp.take_along_axis(values, index, axis=1)


def kernel(
    n, depth, act_hbm, pick_hbm, map_hbm, hidden_hbm, weight_hbm,
    loss_ref, gh_ref, gw_hbm,
    act, pick_own, table_in, meta, hidden, hidden_x, weight, metas, wfull, sendbuf, sendbuf_x, rows, stats, statrep, comb, statown,
    norms, tsums, e_all, g_all, gh_acc, ghsend, ghrecv, gw_ref,
    s_loc, s_hx, r_hx, s_meta, r_meta, s_w, r_w, s_row, r_row, s_rowx, r_rowx, s_fc, r_fc, s_fr, r_fr,
    s_sr, r_sr, s_so, r_so, s_gx, r_gx, s_gc, r_gc, s_gr, r_gr, s_gh, r_gh,
):
    labels, part = weight_hbm.shape
    samples = hidden_hbm.shape[0]
    cols = labels // 4
    o = lax.axis_index("own")
    r = lax.axis_index("rep")
    p1 = r + 1 - 2 * lax.rem(r, 2)
    p2 = lax.rem(r + 2, 4)
    p3 = lax.rem(p1 + 2, 4)
    row_count = n * depth
    pending = []
    local = [
        pltpu.make_async_copy(act_hbm, act, s_loc.at[0]),
        pltpu.make_async_copy(hidden_hbm, hidden, s_loc.at[1]),
        pltpu.make_async_copy(weight_hbm, weight, s_loc.at[2]),
        pltpu.make_async_copy(
            weight_hbm.at[pl.ds(pl.multiple_of(r * cols, cols), cols)],
            wfull.at[:, pl.ds(pl.multiple_of(r * part, part), part)],
            s_loc.at[3],
        ),
        pltpu.make_async_copy(pick_hbm, pick_own, s_loc.at[8]),
        pltpu.make_async_copy(map_hbm, table_in, s_loc.at[9]),
    ]

    def send(src, dst, ssem, rsem, own, rep):
        copy = pltpu.make_async_remote_copy(
            src_ref=src, dst_ref=dst, send_sem=ssem, recv_sem=rsem,
            device_id={"own": own, "rep": rep}, device_id_type=MESH,
        )
        copy.start()
        pending.append(copy)
        return copy

    def at_rows(s):
        return pl.ds(pl.multiple_of(s * depth, depth), depth)

    def at_part(q):
        return pl.ds(pl.multiple_of(q * part, part), part)

    unit = cols // 4
    pieces = ((0, unit), (unit, cols - unit))

    def at_cols(q, start=0, size=None):
        size = cols if size is None else size
        return pl.ds(pl.multiple_of(q * cols + start, unit), size)

    barrier = pltpu.get_barrier_semaphore()
    for k in range(1, n):
        pl.semaphore_signal(barrier, inc=1, device_id={"own": lax.rem(o + k, n), "rep": r}, device_id_type=MESH)
    for q in (p1, p2, p3):
        pl.semaphore_signal(barrier, inc=1, device_id={"own": o, "rep": q}, device_id_type=MESH)
    for c in local:
        c.start()
    local[0].wait()
    local[4].wait()
    local[5].wait()
    meta[0:2, :] = act[...]
    meta[2:3, :] = pick_own[...]
    meta[3:8, :] = jnp.zeros((5, samples), jnp.int32)
    meta[3:4, 0:n] = table_in[...]
    local[1].wait()
    below = lax.broadcasted_iota(jnp.int32, (samples, samples), 0)
    right = lax.broadcasted_iota(jnp.int32, (samples, samples), 1)
    upper = jnp.where(below < right, 1.0, 0.0).astype(BF16)

    def slots(ids):
        table = jnp.broadcast_to(meta[3:4, :], (n, samples))
        return lane_pick(table, jnp.broadcast_to(ids, (n, samples)))[: ids.shape[0]]

    mine = meta[...]
    own_rank = ranks(slots(mine[0:1]), slots(mine[1:2]), n, upper)
    place = lax.broadcasted_iota(jnp.int32, (depth, samples), 0)
    pack = jnp.concatenate(
        [jnp.where(own_rank[b : b + 1] == place, 1.0, 0.0).astype(BF16) for b in range(n)], axis=0
    )
    packed = jnp.dot(pack, hidden[...], preferred_element_type=F32).astype(BF16)
    for b in range(n):
        sendbuf[b] = packed[b * depth : (b + 1) * depth]
    pl.semaphore_wait(barrier, n - 1 + 3)
    hx = send(hidden_hbm, hidden_x, s_hx, r_hx, o, p2)
    row_copies = [
        send(sendbuf.at[lax.rem(o + k, n)], rows.at[at_rows(o), at_part(r)], s_row.at[k - 1], r_row.at[k - 1], lax.rem(o + k, n), r)
        for k in range(1, n)
    ]

    w_copies = [
        send(
            weight_hbm.at[at_cols(q, start, size)], wfull.at[start : start + size, at_part(r)],
            s_w.at[3 * j + i], r_w.at[3 * j + i], o, q,
        )
        for j, (start, size) in enumerate(pieces)
        for i, q in ((1, p2), (2, p3), (0, p1))
    ]
    meta_copies = [
        send(meta, metas.at[o], s_meta.at[k - 1], r_meta.at[k - 1], lax.rem(o + k, n), r)
        for k in range(1, n)
    ]

    rows[at_rows(o), at_part(r)] = sendbuf[o]
    metas[o] = mine

    hx.wait_recv()
    packed_x = jnp.dot(pack, hidden_x[...], preferred_element_type=F32).astype(BF16)
    for b in range(n):
        sendbuf_x[b] = packed_x[b * depth : (b + 1) * depth]
    rowx_copies = [
        send(sendbuf_x.at[lax.rem(o + k, n)], rows.at[at_rows(o), at_part(p2)], s_rowx.at[k - 1], r_rowx.at[k - 1], lax.rem(o + k, n), r)
        for k in range(1, n)
    ]
    rows[at_rows(o), at_part(p2)] = sendbuf_x[o]

    fc, fr = [], []
    for k in range(n):
        s = lax.rem(o - k + n, n)
        if k > 0:
            row_copies[k - 1].wait_recv()
        block = rows.at[at_rows(s), at_part(r)]
        fc.append(send(block, block, s_fc.at[k], r_fc.at[k], o, p1))

    for c in meta_copies:
        c.wait_recv()
    slot0 = slots(metas[:, 0, :])
    slot1 = slots(metas[:, 1, :])
    pick = metas[:, 2, :]
    rank_all = ranks(slot0, slot1, n, upper)
    wanted = jnp.where(pick < labels, slot0, slot1)
    code = jnp.where(wanted == o, jnp.where(pick < labels, pick, pick - labels) + 1, 0)
    code_hi = (code // 64).astype(F32)
    code_lo = (code - (code // 64) * 64).astype(F32)
    lane = lax.broadcasted_iota(jnp.int32, (1, samples), 1)
    sub = lax.broadcasted_iota(jnp.int32, (8, samples), 0)
    bucket_sub = lax.broadcasted_iota(jnp.int32, (n, samples), 0)
    infos = []
    place2 = lax.broadcasted_iota(jnp.int32, (2 * depth, samples), 0)
    for sp in range(n // 2):
        info = jnp.zeros((8, 2 * depth), F32)
        for h in range(2):
            s = 2 * sp + h
            rank_me = jnp.max(
                jnp.where(bucket_sub == o, rank_all[s * n : (s + 1) * n], -1), axis=0, keepdims=True
            )
            member = jnp.where(
                (rank_me >= 0) & (rank_me + h * depth == place2), 1.0, 0.0
            ).astype(BF16)
            facts = jnp.where(
                sub == 0, lane.astype(F32),
                jnp.where(sub == 1, code_hi[s : s + 1], jnp.where(sub == 2, code_lo[s : s + 1], jnp.where(sub == 3, 1.0, 0.0))),
            ).astype(BF16)
            info = info + lax.dot_general(facts, member, NT, preferred_element_type=F32)
        infos.append(info)
    row_index = [x[0:1].astype(jnp.int32) for x in infos]
    row_valid = jnp.concatenate([x[3:4] for x in infos], axis=1) > 0.5
    row_target = jnp.concatenate([(x[1:2] * 64.0 + x[2:3]) for x in infos], axis=1).astype(jnp.int32) - 1

    for k in range(n):
        s = lax.rem(o - k + n, n)
        if k > 0:
            rowx_copies[k - 1].wait_recv()
        block = rows.at[at_rows(s), at_part(p2)]
        fr.append(send(block, block, s_fr.at[k], r_fr.at[k], o, p1))
    for k in range(n):
        fc[k].wait_recv()
    for k in range(n):
        fr[k].wait_recv()
    local[2].wait()
    local[3].wait()

    gx, gc, gr = [], [], []

    def pass_on(c):
        block = e_all.at[at_cols(r, c * unit, unit)]
        gx.append(send(block, block, s_gx.at[c], r_gx.at[c], o, p2))
        gc.append(send(block, block, s_gc.at[c], r_gc.at[c], o, p1))

    tops, sums, targets = [], [], []
    for j, (start, size) in enumerate(pieces):
        for c in w_copies[3 * j : 3 * j + 3]:
            c.wait_recv()
        logits = lax.dot_general(wfull[start : start + size, :], rows[...], NT, preferred_element_type=F32)
        top = jnp.max(logits, axis=0, keepdims=True)
        label_id = lax.broadcasted_iota(jnp.int32, (size, row_count), 0) + (r * cols + start)
        raised = jnp.exp(logits - top)
        e_all[at_cols(r, start, size), :] = raised.astype(BF16)
        if j == 0:
            pass_on(0)
        targets.append(jnp.sum(jnp.where(label_id == row_target, logits, 0.0), axis=0, keepdims=True))
        sums.append(jnp.sum(raised, axis=0, keepdims=True))
        tops.append(top)
    target_sum = targets[0] + targets[1]
    peak = jnp.maximum(tops[0], tops[1])
    lse = peak + jnp.log(sums[0] * jnp.exp(tops[0] - peak) + sums[1] * jnp.exp(tops[1] - peak))
    for sp in range(n // 2):
        stats[sp : sp + 1, :] = lse[:, sp * 128 : (sp + 1) * 128]
        stats[n // 2 + sp : n // 2 + sp + 1, :] = target_sum[:, sp * 128 : (sp + 1) * 128]
        stats[n + sp : n + sp + 1, :] = tops[0][:, sp * 128 : (sp + 1) * 128]
        stats[n + n // 2 + sp : n + n // 2 + sp + 1, :] = tops[1][:, sp * 128 : (sp + 1) * 128]
    sr = [
        send(stats, statrep.at[r], s_sr.at[i], r_sr.at[i], o, q)
        for i, q in ((1, p2), (2, p3), (0, p1))
    ]
    for c in range(1, 4):
        pass_on(c)
    statrep[r] = stats[...]
    for c in sr:
        c.wait_recv()
    parts = [statrep[q, 0:n, :] for q in range(4)]
    high = jnp.maximum(jnp.maximum(parts[0], parts[1]), jnp.maximum(parts[2], parts[3]))
    total = high + jnp.log(sum(jnp.exp(x - high) for x in parts))
    is_lse = lax.broadcasted_iota(jnp.int32, (n, samples), 0) < n // 2
    comb[...] = jnp.where(is_lse, total, sum(parts))
    so = [
        send(comb, statown.at[o], s_so.at[k - 1], r_so.at[k - 1], lax.rem(o + k, n), r)
        for k in range(1, n)
    ]
    statown[o] = comb[...]
    for c in so:
        c.wait_recv()
    norm_rows = []
    for sp in range(n // 2):
        held = statown[:, sp, :]
        pair = []
        for h in range(2):
            s = 2 * sp + h
            rank = rank_all[s * n : (s + 1) * n]
            index = jnp.where(rank >= 0, rank + h * depth, 0)
            value = jnp.where(rank >= 0, lane_pick(held, index), -3.0e38)
            most = jnp.max(value, axis=0, keepdims=True)
            norm = most + jnp.log(jnp.sum(jnp.exp(value - most), axis=0, keepdims=True))
            norms[s : s + 1, :] = norm
            pair.append(
                lane_pick(jnp.broadcast_to(norm, (8, samples)), jnp.broadcast_to(row_index[sp], (8, samples)))[0:1]
            )
        norm_rows.append(jnp.where(lane < depth, pair[0], pair[1]))
    row_norm = jnp.concatenate(norm_rows, axis=1)

    def scale_of(q, j):
        base = n + j * (n // 2)
        high = jnp.concatenate(
            [statrep[pl.ds(q, 1), base + sp : base + sp + 1, :].reshape(1, samples) for sp in range(n // 2)], axis=1
        )
        return jnp.where(row_valid, jnp.exp(high - row_norm), 0.0)

    def gradient(q, start, size):
        at = at_cols(q, start, size)
        ids = lax.broadcasted_iota(jnp.int32, (size, row_count), 0) + (q * cols + start)
        scale = scale_of(q, 0 if start == 0 else 1)
        grad = e_all[at, :].astype(F32) * scale - jnp.where(ids == row_target, 1.0, 0.0)
        g_all[at, :] = grad.astype(BF16)

    def row_term(q, start=0, size=None):
        if size is None:
            for first, length in pieces:
                gradient(q, first, length)
            at = at_cols(q)
        else:
            gradient(q, start, size)
            at = at_cols(q, start, size)
        return lax.dot_general(g_all[at, :], weight[at, :], TN, preferred_element_type=F32)

    def weight_term(q, i):
        gw_ref[at_cols(q), :] = jnp.dot(
            g_all[at_cols(q), :], rows[:, at_part(r)], preferred_element_type=F32
        ).astype(BF16)
        out = pltpu.make_async_copy(gw_ref.at[at_cols(q)], gw_hbm.at[at_cols(q)], s_loc.at[4 + i])
        out.start()
        outs.append(out)

    outs = []
    gh_acc[...] = row_term(r)
    for c in range(4):
        gc[c].wait_recv()
    gh_acc[...] += row_term(p1)

    for sp in range(n // 2):
        held = statown[:, n // 2 + sp, :]
        for h in range(2):
            s = 2 * sp + h
            rank = rank_all[s * n : (s + 1) * n]
            index = jnp.where(rank >= 0, rank + h * depth, 0)
            value = jnp.where(rank >= 0, lane_pick(held, index), 0.0)
            tsums[s : s + 1, :] = jnp.sum(value, axis=0, keepdims=True)
    loss_ref[...] = norms[pl.ds(o, 1), :] - tsums[pl.ds(o, 1), :]

    weight_term(r, 0)
    weight_term(p1, 1)
    for c in range(4):
        gx[c].wait_recv()
        block = e_all.at[at_cols(p2, c * unit, unit)]
        gr.append(send(block, block, s_gr.at[c], r_gr.at[c], o, p1))
        gh_acc[...] += row_term(p2, c * unit, unit)
    for c in range(4):
        gr[c].wait_recv()
    ghsend[...] = (gh_acc[...] + row_term(p3)).astype(BF16)
    back = [
        send(ghsend.at[at_rows(lax.rem(o + k, n))], ghrecv.at[at_rows(o)], s_gh.at[k - 1], r_gh.at[k - 1], lax.rem(o + k, n), r)
        for k in range(1, n)
    ]
    ghrecv[at_rows(o), :] = ghsend[at_rows(o), :]
    weight_term(p2, 2)
    weight_term(p3, 3)
    for c in back:
        c.wait_recv()
    gh_ref[...] = lax.dot_general(pack, ghrecv[...], TN, preferred_element_type=F32)
    for c in pending:
        c.wait_send()
    for c in outs:
        c.wait()


def finish(loss_in, gh_in, gw_in, loss_out, gh_out, gw_out, loss_v, gh_v, gw_v, sem_in, sem_out):
    step = gw_in.shape[0] // 4
    moves = [(loss_in, loss_v, loss_out), (gh_in, gh_v, gh_out)]
    for i in range(4):
        at = pl.ds(i * step, step)
        moves.append((gw_in.at[at], gw_v.at[at], gw_out.at[at]))
    ins = [pltpu.make_async_copy(a, b, sem_in.at[i]) for i, (a, b, c) in enumerate(moves)]
    outs = [pltpu.make_async_copy(b, c, sem_out.at[i]) for i, (a, b, c) in enumerate(moves)]
    for c in ins:
        c.start()
    for c, d in zip(ins, outs):
        c.wait()
        d.start()
    for c in outs:
        c.wait()


def fused(hidden, weight, bucket_map, active, label_pick):
    samples, part = hidden.shape
    labels = weight.shape[1]
    n = bucket_map.shape[0]
    depth = 2 * samples * active.shape[1] // n
    cols = labels // 4
    row_count = n * depth
    vmem = pl.BlockSpec(memory_space=pltpu.VMEM)
    dma = pltpu.SemaphoreType.DMA
    sems = [dma((10,)), dma, dma]
    for count in (n - 1, 6, n - 1, n - 1, n, n, 3, n - 1, 4, 4, 4, n - 1):
        sems += [dma((count,)), dma((count,))]
    hbm = pl.BlockSpec(memory_space=pltpu.HBM)
    loss, grad_hidden, grad_weight = pl.pallas_call(
        functools.partial(kernel, n, depth),
        out_shape=(
            jax.ShapeDtypeStruct((1, samples), F32),
            jax.ShapeDtypeStruct((samples, part), F32),
            jax.ShapeDtypeStruct((labels, part), BF16),
        ),
        in_specs=[hbm] * 5,
        out_specs=(vmem, vmem, hbm),
        scratch_shapes=[
            pltpu.VMEM((2, samples), jnp.int32),
            pltpu.VMEM((1, samples), jnp.int32),
            pltpu.VMEM((1, n), jnp.int32),
            pltpu.VMEM((8, samples), jnp.int32),
            pltpu.VMEM((samples, part), BF16),
            pltpu.VMEM((samples, part), BF16),
            pltpu.VMEM((labels, part), BF16),
            pltpu.VMEM((n, 8, samples), jnp.int32),
            pltpu.VMEM((cols, 4 * part), BF16),
            pltpu.VMEM((n, depth, part), BF16),
            pltpu.VMEM((n, depth, part), BF16),
            pltpu.VMEM((row_count, 4 * part), BF16),
            pltpu.VMEM((2 * n, samples), F32),
            pltpu.VMEM((4, 2 * n, samples), F32),
            pltpu.VMEM((n, samples), F32),
            pltpu.VMEM((n, n, samples), F32),
            pltpu.VMEM((n, samples), F32),
            pltpu.VMEM((n, samples), F32),
            pltpu.VMEM((labels, row_count), BF16),
            pltpu.VMEM((labels, row_count), BF16),
            pltpu.VMEM((row_count, part), F32),
            pltpu.VMEM((row_count, part), BF16),
            pltpu.VMEM((row_count, part), BF16),
            pltpu.VMEM((labels, part), BF16),
        ] + sems,
        compiler_params=pltpu.CompilerParams(
            collective_id=0, has_side_effects=True, vmem_limit_bytes=60 * 1024 * 1024
        ),
    )(active.T, label_pick[None], bucket_map[None], hidden, weight[0])
    loss, grad_hidden, grad_weight = pl.pallas_call(
        finish,
        out_shape=(
            jax.ShapeDtypeStruct((1, samples), F32),
            jax.ShapeDtypeStruct((samples, part), F32),
            jax.ShapeDtypeStruct((labels, part), BF16),
        ),
        in_specs=[hbm] * 3,
        out_specs=(hbm, hbm, hbm),
        scratch_shapes=[
            pltpu.VMEM((1, samples), F32),
            pltpu.VMEM((samples, part), F32),
            pltpu.VMEM((labels, part), BF16),
            dma((6,)),
            dma((6,)),
        ],
        compiler_params=pltpu.CompilerParams(vmem_limit_bytes=60 * 1024 * 1024),
    )(loss, grad_hidden, grad_weight)
    return loss[0], grad_hidden, grad_weight[None]


def body(hidden, weight, bucket_map, active, label_pick):
    samp_count = hidden.shape[0]
    bucket_dev, label_count, feature_part = weight.shape
    picks = active.shape[1]
    bucket_total = bucket_map.shape[0]
    owner_count = lax.axis_size("own")
    slot_depth = max(2, 2 * samp_count * picks // bucket_total)
    pair_count = samp_count * picks
    slots_total = bucket_total * slot_depth
    row_count = owner_count * slot_depth
    pair_bucket = active.reshape(pair_count)
    bucket_iota = lax.broadcasted_iota(jnp.int32, (pair_count, bucket_total), 1)
    slot_index = jnp.sum(
        jnp.where(pair_bucket[:, None] == bucket_iota, bucket_map[None, :], 0), axis=1
    )
    slot_hits = (slot_index[:, None] == bucket_iota).astype(jnp.int32)
    earlier = jnp.cumsum(slot_hits, axis=0) - slot_hits
    rank_within = jnp.sum(earlier * slot_hits, axis=1)
    position = slot_index * slot_depth + rank_within
    pair_index = jnp.arange(pair_count, dtype=jnp.int32)
    pick_value = jnp.repeat(label_pick, picks)
    target_pair = jnp.where(
        pick_value // label_count == pair_index % picks, pick_value % label_count, -1
    )
    width_sent = hidden.shape[1]
    pair_rows = jnp.repeat(hidden, picks, axis=0)
    send_rows = jnp.zeros((slots_total, width_sent), jnp.bfloat16).at[position].set(pair_rows)
    send_target = jnp.full((slots_total,), -1, jnp.int32).at[position].set(target_pair)
    got_rows, got_target = (
        lax.all_to_all(
            send_rows.reshape(owner_count, bucket_dev * slot_depth, width_sent),
            "own",
            split_axis=0,
            concat_axis=0,
            tiled=True,
        ),
        lax.all_to_all(
            send_target.reshape(owner_count, bucket_dev * slot_depth),
            "own",
            split_axis=0,
            concat_axis=0,
            tiled=True,
        ),
    )
    received = got_rows.reshape(owner_count, bucket_dev, slot_depth, width_sent).transpose(
        1, 0, 2, 3
    )
    received = received.reshape(bucket_dev, row_count, width_sent)
    target_col = (
        got_target.reshape(owner_count, bucket_dev, slot_depth)
        .transpose(1, 0, 2)
        .reshape(bucket_dev, row_count)
    )
    partial_value = jnp.einsum("brd,bcd->brc", received, weight, preferred_element_type=jnp.float32)
    logits = lax.psum(partial_value, "rep")
    columns = lax.broadcasted_iota(jnp.int32, (1, 1, label_count), 2)
    row_max = jnp.max(logits, axis=2)
    row_sum = jnp.sum(jnp.exp(logits - row_max[..., None]), axis=2)
    row_target = jnp.sum(jnp.where(columns == target_col[..., None], logits, 0.0), axis=2)

    def to_sources(values):
        return (
            values.reshape(bucket_dev, owner_count, slot_depth)
            .transpose(1, 0, 2)
            .reshape(owner_count, bucket_dev * slot_depth)
        )

    back_max, back_sum, back_target = (
        lax.all_to_all(to_sources(row_max), "own", split_axis=0, concat_axis=0, tiled=True),
        lax.all_to_all(to_sources(row_sum), "own", split_axis=0, concat_axis=0, tiled=True),
        lax.all_to_all(to_sources(row_target), "own", split_axis=0, concat_axis=0, tiled=True),
    )
    pair_max = back_max.reshape(slots_total)[position].reshape(samp_count, picks)
    pair_sum = back_sum.reshape(slots_total)[position].reshape(samp_count, picks)
    pair_target = back_target.reshape(slots_total)[position].reshape(samp_count, picks)
    peak_max = jnp.max(pair_max, axis=1)
    norm_sum = jnp.sum(pair_sum * jnp.exp(pair_max - peak_max[:, None]), axis=1)
    log_norm = peak_max + jnp.log(norm_sum)
    sample_loss = log_norm - jnp.sum(pair_target, axis=1)
    send_norm = jnp.zeros((slots_total,), jnp.float32).at[position].set(jnp.repeat(log_norm, picks))
    got_norm = lax.all_to_all(
        send_norm.reshape(owner_count, bucket_dev * slot_depth),
        "own",
        split_axis=0,
        concat_axis=0,
        tiled=True,
    )
    row_norm = (
        got_norm.reshape(owner_count, bucket_dev, slot_depth)
        .transpose(1, 0, 2)
        .reshape(bucket_dev, row_count)
    )
    onehot = (columns == target_col[..., None]).astype(jnp.float32)
    grad_logits = (jnp.exp(logits - row_norm[..., None]) - onehot).astype(jnp.bfloat16)
    grad_weight = jnp.einsum(
        "brc,brd->bcd", grad_logits, received, preferred_element_type=jnp.float32
    ).astype(jnp.bfloat16)
    row_grads = jnp.einsum("brc,bcd->brd", grad_logits, weight, preferred_element_type=jnp.float32)
    send_grads = row_grads.reshape(bucket_dev, owner_count, slot_depth, feature_part).transpose(
        1, 0, 2, 3
    )
    send_grads = send_grads.reshape(owner_count, bucket_dev * slot_depth, feature_part)
    got_grads = lax.all_to_all(send_grads, "own", split_axis=0, concat_axis=0, tiled=True)
    pair_grads = got_grads.reshape(slots_total, feature_part)[position].reshape(
        samp_count, picks, feature_part
    )
    grad_hidden = jnp.sum(pair_grads, axis=1)
    return (sample_loss, grad_hidden, grad_weight)


def choose(hidden, weight, bucket_map, active, label_pick):
    samples, picks = active.shape
    buckets = bucket_map.shape[0]
    depth = 2 * samples * picks // buckets
    fits = (
        weight.shape[0] == 1
        and lax.axis_size("rep") == 4
        and buckets == 8
        and picks == 2
        and samples == 128
        and 2 * depth == samples
        and weight.shape[1] % 512 == 0
        and hidden.shape[1] % 128 == 0
    )
    run = fused if fits else body
    return run(hidden, weight, bucket_map, active, label_pick)


def solution(mesh):
    in_specs = (P("own", "rep"), P("own", None, "rep"), P(), P("own", None), P("own"))
    out_specs = (P("own"), P("own", "rep"), P("own", None, "rep"))
    return jax.shard_map(choose, mesh=mesh, in_specs=in_specs, out_specs=out_specs, check_vma=False)
```

```python
import functools
import jax
import jax.numpy as jnp
from jax import lax
from jax.experimental import pallas as pl
from jax.experimental.pallas import tpu as pltpu
from jax.sharding import PartitionSpec as P

MESH = pl.DeviceIdType.MESH
F32 = jnp.float32
BF16 = jnp.bfloat16
NT = (((1,), (1,)), ((), ()))
TN = (((0,), (0,)), ((), ()))


def ranks(slot0, slot1, buckets, upper):
    sources, samples = slot0.shape
    bucket = lax.broadcasted_iota(jnp.int32, (buckets, samples), 0)
    hits = [
        jnp.where((slot0[s : s + 1] == bucket) | (slot1[s : s + 1] == bucket), 1.0, 0.0)
        for s in range(sources)
    ]
    hits = jnp.concatenate(hits, axis=0) if sources > 1 else hits[0]
    earlier = jnp.dot(hits.astype(BF16), upper, preferred_element_type=F32)
    return jnp.where(hits > 0.5, earlier, -1.0).astype(jnp.int32)


def lane_pick(values, index):
    return jnp.take_along_axis(values, index, axis=1)


def kernel(
    n, depth, act_hbm, pick_hbm, map_hbm, hidden_hbm, weight_hbm,
    loss_ref, gh_ref, gw_hbm,
    act, pick_own, table_in, meta, hidden, hidden_x, weight, metas, wfull, sendbuf, sendbuf_x, rows, stats, statrep, comb, statown,
    norms, tsums, e_all, g_all, gh_acc, ghsend, ghrecv, gw_ref,
    s_loc, s_hx, r_hx, s_meta, r_meta, s_w, r_w, s_row, r_row, s_rowx, r_rowx, s_fc, r_fc, s_fr, r_fr,
    s_sr, r_sr, s_so, r_so, s_gx, r_gx, s_gc, r_gc, s_gr, r_gr, s_gh, r_gh,
):
    labels, part = weight_hbm.shape
    samples = hidden_hbm.shape[0]
    cols = labels // 4
    o = lax.axis_index("own")
    r = lax.axis_index("rep")
    p1 = r + 1 - 2 * lax.rem(r, 2)
    p2 = lax.rem(r + 2, 4)
    p3 = lax.rem(p1 + 2, 4)
    row_count = n * depth
    pending = []
    local = [
        pltpu.make_async_copy(act_hbm, act, s_loc.at[0]),
        pltpu.make_async_copy(hidden_hbm, hidden, s_loc.at[1]),
        pltpu.make_async_copy(weight_hbm, weight, s_loc.at[2]),
        pltpu.make_async_copy(
            weight_hbm.at[pl.ds(pl.multiple_of(r * cols, cols), cols)],
            wfull.at[:, pl.ds(pl.multiple_of(r * part, part), part)],
            s_loc.at[3],
        ),
        pltpu.make_async_copy(pick_hbm, pick_own, s_loc.at[8]),
        pltpu.make_async_copy(map_hbm, table_in, s_loc.at[9]),
    ]

    def send(src, dst, ssem, rsem, own, rep):
        copy = pltpu.make_async_remote_copy(
            src_ref=src, dst_ref=dst, send_sem=ssem, recv_sem=rsem,
            device_id={"own": own, "rep": rep}, device_id_type=MESH,
        )
        copy.start()
        pending.append(copy)
        return copy

    def at_rows(s):
        return pl.ds(pl.multiple_of(s * depth, depth), depth)

    def at_part(q):
        return pl.ds(pl.multiple_of(q * part, part), part)

    unit = cols // 4
    pieces = ((0, unit), (unit, cols - unit))

    def at_cols(q, start=0, size=None):
        size = cols if size is None else size
        return pl.ds(pl.multiple_of(q * cols + start, unit), size)

    barrier = pltpu.get_barrier_semaphore()
    for k in range(1, n):
        pl.semaphore_signal(barrier, inc=1, device_id={"own": lax.rem(o + k, n), "rep": r}, device_id_type=MESH)
    for q in (p1, p2, p3):
        pl.semaphore_signal(barrier, inc=1, device_id={"own": o, "rep": q}, device_id_type=MESH)
    for c in local:
        c.start()
    local[0].wait()
    local[4].wait()
    local[5].wait()
    meta[0:2, :] = act[...]
    meta[2:3, :] = pick_own[...]
    meta[3:8, :] = jnp.zeros((5, samples), jnp.int32)
    meta[3:4, 0:n] = table_in[...]
    local[1].wait()
    below = lax.broadcasted_iota(jnp.int32, (samples, samples), 0)
    right = lax.broadcasted_iota(jnp.int32, (samples, samples), 1)
    upper = jnp.where(below < right, 1.0, 0.0).astype(BF16)

    def slots(ids):
        table = jnp.broadcast_to(meta[3:4, :], (n, samples))
        return lane_pick(table, jnp.broadcast_to(ids, (n, samples)))[: ids.shape[0]]

    mine = meta[...]
    own_rank = ranks(slots(mine[0:1]), slots(mine[1:2]), n, upper)
    place = lax.broadcasted_iota(jnp.int32, (depth, samples), 0)
    pack = jnp.concatenate(
        [jnp.where(own_rank[b : b + 1] == place, 1.0, 0.0).astype(BF16) for b in range(n)], axis=0
    )
    packed = jnp.dot(pack, hidden[...], preferred_element_type=F32).astype(BF16)
    for b in range(n):
        sendbuf[b] = packed[b * depth : (b + 1) * depth]
    pl.semaphore_wait(barrier, n - 1 + 3)
    hx = send(hidden_hbm, hidden_x, s_hx, r_hx, o, p2)
    row_copies = [
        send(sendbuf.at[lax.rem(o + k, n)], rows.at[at_rows(o), at_part(r)], s_row.at[k - 1], r_row.at[k - 1], lax.rem(o + k, n), r)
        for k in range(1, n)
    ]

    w_copies = [
        send(
            weight_hbm.at[at_cols(q, start, size)], wfull.at[start : start + size, at_part(r)],
            s_w.at[3 * j + i], r_w.at[3 * j + i], o, q,
        )
        for j, (start, size) in enumerate(pieces)
        for i, q in ((1, p2), (2, p3), (0, p1))
    ]
    meta_copies = [
        send(meta, metas.at[o], s_meta.at[k - 1], r_meta.at[k - 1], lax.rem(o + k, n), r)
        for k in range(1, n)
    ]

    rows[at_rows(o), at_part(r)] = sendbuf[o]
    metas[o] = mine

    hx.wait_recv()
    packed_x = jnp.dot(pack, hidden_x[...], preferred_element_type=F32).astype(BF16)
    for b in range(n):
        sendbuf_x[b] = packed_x[b * depth : (b + 1) * depth]
    rowx_copies = [
        send(sendbuf_x.at[lax.rem(o + k, n)], rows.at[at_rows(o), at_part(p2)], s_rowx.at[k - 1], r_rowx.at[k - 1], lax.rem(o + k, n), r)
        for k in range(1, n)
    ]
    rows[at_rows(o), at_part(p2)] = sendbuf_x[o]

    fc, fr = [], []
    for k in range(n):
        s = lax.rem(o - k + n, n)
        if k > 0:
            row_copies[k - 1].wait_recv()
        block = rows.at[at_rows(s), at_part(r)]
        fc.append(send(block, block, s_fc.at[k], r_fc.at[k], o, p1))

    for c in meta_copies:
        c.wait_recv()
    slot0 = slots(metas[:, 0, :])
    slot1 = slots(metas[:, 1, :])
    pick = metas[:, 2, :]
    rank_all = ranks(slot0, slot1, n, upper)
    wanted = jnp.where(pick < labels, slot0, slot1)
    code = jnp.where(wanted == o, jnp.where(pick < labels, pick, pick - labels) + 1, 0)
    code_hi = (code // 64).astype(F32)
    code_lo = (code - (code // 64) * 64).astype(F32)
    lane = lax.broadcasted_iota(jnp.int32, (1, samples), 1)
    sub = lax.broadcasted_iota(jnp.int32, (8, samples), 0)
    bucket_sub = lax.broadcasted_iota(jnp.int32, (n, samples), 0)
    infos = []
    place2 = lax.broadcasted_iota(jnp.int32, (2 * depth, samples), 0)
    for sp in range(n // 2):
        info = jnp.zeros((8, 2 * depth), F32)
        for h in range(2):
            s = 2 * sp + h
            rank_me = jnp.max(
                jnp.where(bucket_sub == o, rank_all[s * n : (s + 1) * n], -1), axis=0, keepdims=True
            )
            member = jnp.where(
                (rank_me >= 0) & (rank_me + h * depth == place2), 1.0, 0.0
            ).astype(BF16)
            facts = jnp.where(
                sub == 0, lane.astype(F32),
                jnp.where(sub == 1, code_hi[s : s + 1], jnp.where(sub == 2, code_lo[s : s + 1], jnp.where(sub == 3, 1.0, 0.0))),
            ).astype(BF16)
            info = info + lax.dot_general(facts, member, NT, preferred_element_type=F32)
        infos.append(info)
    row_index = [x[0:1].astype(jnp.int32) for x in infos]
    row_valid = jnp.concatenate([x[3:4] for x in infos], axis=1) > 0.5
    row_target = jnp.concatenate([(x[1:2] * 64.0 + x[2:3]) for x in infos], axis=1).astype(jnp.int32) - 1

    for k in range(n):
        s = lax.rem(o - k + n, n)
        if k > 0:
            rowx_copies[k - 1].wait_recv()
        block = rows.at[at_rows(s), at_part(p2)]
        fr.append(send(block, block, s_fr.at[k], r_fr.at[k], o, p1))
    for k in range(n):
        fc[k].wait_recv()
    for k in range(n):
        fr[k].wait_recv()
    local[2].wait()
    local[3].wait()

    gx, gc, gr = [], [], []

    def pass_on(c):
        block = e_all.at[at_cols(r, c * unit, unit)]
        gx.append(send(block, block, s_gx.at[c], r_gx.at[c], o, p2))
        gc.append(send(block, block, s_gc.at[c], r_gc.at[c], o, p1))

    tops, sums, targets = [], [], []
    for j, (start, size) in enumerate(pieces):
        for c in w_copies[3 * j : 3 * j + 3]:
            c.wait_recv()
        logits = lax.dot_general(wfull[start : start + size, :], rows[...], NT, preferred_element_type=F32)
        top = jnp.max(logits, axis=0, keepdims=True)
        label_id = lax.broadcasted_iota(jnp.int32, (size, row_count), 0) + (r * cols + start)
        raised = jnp.exp(logits - top)
        e_all[at_cols(r, start, size), :] = raised.astype(BF16)
        if j == 0:
            pass_on(0)
        targets.append(jnp.sum(jnp.where(label_id == row_target, logits, 0.0), axis=0, keepdims=True))
        sums.append(jnp.sum(raised, axis=0, keepdims=True))
        tops.append(top)
    target_sum = targets[0] + targets[1]
    peak = jnp.maximum(tops[0], tops[1])
    lse = peak + jnp.log(sums[0] * jnp.exp(tops[0] - peak) + sums[1] * jnp.exp(tops[1] - peak))
    for sp in range(n // 2):
        stats[sp : sp + 1, :] = lse[:, sp * 128 : (sp + 1) * 128]
        stats[n // 2 + sp : n // 2 + sp + 1, :] = target_sum[:, sp * 128 : (sp + 1) * 128]
        stats[n + sp : n + sp + 1, :] = tops[0][:, sp * 128 : (sp + 1) * 128]
        stats[n + n // 2 + sp : n + n // 2 + sp + 1, :] = tops[1][:, sp * 128 : (sp + 1) * 128]
    sr = [
        send(stats, statrep.at[r], s_sr.at[i], r_sr.at[i], o, q)
        for i, q in ((1, p2), (2, p3), (0, p1))
    ]
    for c in range(1, 4):
        pass_on(c)
    statrep[r] = stats[...]
    for c in sr:
        c.wait_recv()
    parts = [statrep[q, 0:n, :] for q in range(4)]
    high = jnp.maximum(jnp.maximum(parts[0], parts[1]), jnp.maximum(parts[2], parts[3]))
    total = high + jnp.log(sum(jnp.exp(x - high) for x in parts))
    is_lse = lax.broadcasted_iota(jnp.int32, (n, samples), 0) < n // 2
    comb[...] = jnp.where(is_lse, total, sum(parts))
    so = [
        send(comb, statown.at[o], s_so.at[k - 1], r_so.at[k - 1], lax.rem(o + k, n), r)
        for k in range(1, n)
    ]
    statown[o] = comb[...]
    for c in so:
        c.wait_recv()
    norm_rows = []
    for sp in range(n // 2):
        held = statown[:, sp, :]
        pair = []
        for h in range(2):
            s = 2 * sp + h
            rank = rank_all[s * n : (s + 1) * n]
            index = jnp.where(rank >= 0, rank + h * depth, 0)
            value = jnp.where(rank >= 0, lane_pick(held, index), -3.0e38)
            most = jnp.max(value, axis=0, keepdims=True)
            norm = most + jnp.log(jnp.sum(jnp.exp(value - most), axis=0, keepdims=True))
            norms[s : s + 1, :] = norm
            pair.append(
                lane_pick(jnp.broadcast_to(norm, (8, samples)), jnp.broadcast_to(row_index[sp], (8, samples)))[0:1]
            )
        norm_rows.append(jnp.where(lane < depth, pair[0], pair[1]))
    row_norm = jnp.concatenate(norm_rows, axis=1)

    def scale_of(q, j):
        base = n + j * (n // 2)
        high = jnp.concatenate(
            [statrep[pl.ds(q, 1), base + sp : base + sp + 1, :].reshape(1, samples) for sp in range(n // 2)], axis=1
        )
        return jnp.where(row_valid, jnp.exp(high - row_norm), 0.0)

    def gradient(q, start, size):
        at = at_cols(q, start, size)
        ids = lax.broadcasted_iota(jnp.int32, (size, row_count), 0) + (q * cols + start)
        scale = scale_of(q, 0 if start == 0 else 1)
        grad = e_all[at, :].astype(F32) * scale - jnp.where(ids == row_target, 1.0, 0.0)
        g_all[at, :] = grad.astype(BF16)

    def row_term(q, start=0, size=None):
        if size is None:
            for first, length in pieces:
                gradient(q, first, length)
            at = at_cols(q)
        else:
            gradient(q, start, size)
            at = at_cols(q, start, size)
        return lax.dot_general(g_all[at, :], weight[at, :], TN, preferred_element_type=F32)

    def weight_term(q, i):
        gw_ref[at_cols(q), :] = jnp.dot(
            g_all[at_cols(q), :], rows[:, at_part(r)], preferred_element_type=F32
        ).astype(BF16)
        out = pltpu.make_async_copy(gw_ref.at[at_cols(q)], gw_hbm.at[at_cols(q)], s_loc.at[4 + i])
        out.start()
        outs.append(out)

    outs = []
    gh_acc[...] = row_term(r)
    for c in range(4):
        gc[c].wait_recv()
    gh_acc[...] += row_term(p1)

    for sp in range(n // 2):
        held = statown[:, n // 2 + sp, :]
        for h in range(2):
            s = 2 * sp + h
            rank = rank_all[s * n : (s + 1) * n]
            index = jnp.where(rank >= 0, rank + h * depth, 0)
            value = jnp.where(rank >= 0, lane_pick(held, index), 0.0)
            tsums[s : s + 1, :] = jnp.sum(value, axis=0, keepdims=True)
    loss_ref[...] = norms[pl.ds(o, 1), :] - tsums[pl.ds(o, 1), :]

    weight_term(r, 0)
    weight_term(p1, 1)
    for c in range(4):
        gx[c].wait_recv()
        block = e_all.at[at_cols(p2, c * unit, unit)]
        gr.append(send(block, block, s_gr.at[c], r_gr.at[c], o, p1))
        gh_acc[...] += row_term(p2, c * unit, unit)
        if c > 0:
            gr[c - 1].wait_recv()
            gh_acc[...] += row_term(p3, (c - 1) * unit, unit)
    gr[3].wait_recv()
    ghsend[...] = (gh_acc[...] + row_term(p3, 3 * unit, unit)).astype(BF16)
    back = [
        send(ghsend.at[at_rows(lax.rem(o + k, n))], ghrecv.at[at_rows(o)], s_gh.at[k - 1], r_gh.at[k - 1], lax.rem(o + k, n), r)
        for k in range(1, n)
    ]
    ghrecv[at_rows(o), :] = ghsend[at_rows(o), :]
    weight_term(p2, 2)
    weight_term(p3, 3)
    for c in back:
        c.wait_recv()
    gh_ref[...] = lax.dot_general(pack, ghrecv[...], TN, preferred_element_type=F32)
    for c in pending:
        c.wait_send()
    for c in outs:
        c.wait()


def finish(loss_in, gh_in, gw_in, loss_out, gh_out, gw_out, loss_v, gh_v, gw_v, sem_in, sem_out):
    step = gw_in.shape[0] // 4
    moves = [(loss_in, loss_v, loss_out), (gh_in, gh_v, gh_out)]
    for i in range(4):
        at = pl.ds(i * step, step)
        moves.append((gw_in.at[at], gw_v.at[at], gw_out.at[at]))
    ins = [pltpu.make_async_copy(a, b, sem_in.at[i]) for i, (a, b, c) in enumerate(moves)]
    outs = [pltpu.make_async_copy(b, c, sem_out.at[i]) for i, (a, b, c) in enumerate(moves)]
    for c in ins:
        c.start()
    for c, d in zip(ins, outs):
        c.wait()
        d.start()
    for c in outs:
        c.wait()


def fused(hidden, weight, bucket_map, active, label_pick):
    samples, part = hidden.shape
    labels = weight.shape[1]
    n = bucket_map.shape[0]
    depth = 2 * samples * active.shape[1] // n
    cols = labels // 4
    row_count = n * depth
    vmem = pl.BlockSpec(memory_space=pltpu.VMEM)
    dma = pltpu.SemaphoreType.DMA
    sems = [dma((10,)), dma, dma]
    for count in (n - 1, 6, n - 1, n - 1, n, n, 3, n - 1, 4, 4, 4, n - 1):
        sems += [dma((count,)), dma((count,))]
    hbm = pl.BlockSpec(memory_space=pltpu.HBM)
    loss, grad_hidden, grad_weight = pl.pallas_call(
        functools.partial(kernel, n, depth),
        out_shape=(
            jax.ShapeDtypeStruct((1, samples), F32),
            jax.ShapeDtypeStruct((samples, part), F32),
            jax.ShapeDtypeStruct((labels, part), BF16),
        ),
        in_specs=[hbm] * 5,
        out_specs=(vmem, vmem, hbm),
        scratch_shapes=[
            pltpu.VMEM((2, samples), jnp.int32),
            pltpu.VMEM((1, samples), jnp.int32),
            pltpu.VMEM((1, n), jnp.int32),
            pltpu.VMEM((8, samples), jnp.int32),
            pltpu.VMEM((samples, part), BF16),
            pltpu.VMEM((samples, part), BF16),
            pltpu.VMEM((labels, part), BF16),
            pltpu.VMEM((n, 8, samples), jnp.int32),
            pltpu.VMEM((cols, 4 * part), BF16),
            pltpu.VMEM((n, depth, part), BF16),
            pltpu.VMEM((n, depth, part), BF16),
            pltpu.VMEM((row_count, 4 * part), BF16),
            pltpu.VMEM((2 * n, samples), F32),
            pltpu.VMEM((4, 2 * n, samples), F32),
            pltpu.VMEM((n, samples), F32),
            pltpu.VMEM((n, n, samples), F32),
            pltpu.VMEM((n, samples), F32),
            pltpu.VMEM((n, samples), F32),
            pltpu.VMEM((labels, row_count), BF16),
            pltpu.VMEM((labels, row_count), BF16),
            pltpu.VMEM((row_count, part), F32),
            pltpu.VMEM((row_count, part), BF16),
            pltpu.VMEM((row_count, part), BF16),
            pltpu.VMEM((labels, part), BF16),
        ] + sems,
        compiler_params=pltpu.CompilerParams(
            collective_id=0, has_side_effects=True, vmem_limit_bytes=60 * 1024 * 1024
        ),
    )(active.T, label_pick[None], bucket_map[None], hidden, weight[0])
    loss, grad_hidden, grad_weight = pl.pallas_call(
        finish,
        out_shape=(
            jax.ShapeDtypeStruct((1, samples), F32),
            jax.ShapeDtypeStruct((samples, part), F32),
            jax.ShapeDtypeStruct((labels, part), BF16),
        ),
        in_specs=[hbm] * 3,
        out_specs=(hbm, hbm, hbm),
        scratch_shapes=[
            pltpu.VMEM((1, samples), F32),
            pltpu.VMEM((samples, part), F32),
            pltpu.VMEM((labels, part), BF16),
            dma((6,)),
            dma((6,)),
        ],
        compiler_params=pltpu.CompilerParams(vmem_limit_bytes=60 * 1024 * 1024),
    )(loss, grad_hidden, grad_weight)
    return loss[0], grad_hidden, grad_weight[None]


def body(hidden, weight, bucket_map, active, label_pick):
    samp_count = hidden.shape[0]
    bucket_dev, label_count, feature_part = weight.shape
    picks = active.shape[1]
    bucket_total = bucket_map.shape[0]
    owner_count = lax.axis_size("own")
    slot_depth = max(2, 2 * samp_count * picks // bucket_total)
    pair_count = samp_count * picks
    slots_total = bucket_total * slot_depth
    row_count = owner_count * slot_depth
    pair_bucket = active.reshape(pair_count)
    bucket_iota = lax.broadcasted_iota(jnp.int32, (pair_count, bucket_total), 1)
    slot_index = jnp.sum(
        jnp.where(pair_bucket[:, None] == bucket_iota, bucket_map[None, :], 0), axis=1
    )
    slot_hits = (slot_index[:, None] == bucket_iota).astype(jnp.int32)
    earlier = jnp.cumsum(slot_hits, axis=0) - slot_hits
    rank_within = jnp.sum(earlier * slot_hits, axis=1)
    position = slot_index * slot_depth + rank_within
    pair_index = jnp.arange(pair_count, dtype=jnp.int32)
    pick_value = jnp.repeat(label_pick, picks)
    target_pair = jnp.where(
        pick_value // label_count == pair_index % picks, pick_value % label_count, -1
    )
    width_sent = hidden.shape[1]
    pair_rows = jnp.repeat(hidden, picks, axis=0)
    send_rows = jnp.zeros((slots_total, width_sent), jnp.bfloat16).at[position].set(pair_rows)
    send_target = jnp.full((slots_total,), -1, jnp.int32).at[position].set(target_pair)
    got_rows, got_target = (
        lax.all_to_all(
            send_rows.reshape(owner_count, bucket_dev * slot_depth, width_sent),
            "own",
            split_axis=0,
            concat_axis=0,
            tiled=True,
        ),
        lax.all_to_all(
            send_target.reshape(owner_count, bucket_dev * slot_depth),
            "own",
            split_axis=0,
            concat_axis=0,
            tiled=True,
        ),
    )
    received = got_rows.reshape(owner_count, bucket_dev, slot_depth, width_sent).transpose(
        1, 0, 2, 3
    )
    received = received.reshape(bucket_dev, row_count, width_sent)
    target_col = (
        got_target.reshape(owner_count, bucket_dev, slot_depth)
        .transpose(1, 0, 2)
        .reshape(bucket_dev, row_count)
    )
    partial_value = jnp.einsum("brd,bcd->brc", received, weight, preferred_element_type=jnp.float32)
    logits = lax.psum(partial_value, "rep")
    columns = lax.broadcasted_iota(jnp.int32, (1, 1, label_count), 2)
    row_max = jnp.max(logits, axis=2)
    row_sum = jnp.sum(jnp.exp(logits - row_max[..., None]), axis=2)
    row_target = jnp.sum(jnp.where(columns == target_col[..., None], logits, 0.0), axis=2)

    def to_sources(values):
        return (
            values.reshape(bucket_dev, owner_count, slot_depth)
            .transpose(1, 0, 2)
            .reshape(owner_count, bucket_dev * slot_depth)
        )

    back_max, back_sum, back_target = (
        lax.all_to_all(to_sources(row_max), "own", split_axis=0, concat_axis=0, tiled=True),
        lax.all_to_all(to_sources(row_sum), "own", split_axis=0, concat_axis=0, tiled=True),
        lax.all_to_all(to_sources(row_target), "own", split_axis=0, concat_axis=0, tiled=True),
    )
    pair_max = back_max.reshape(slots_total)[position].reshape(samp_count, picks)
    pair_sum = back_sum.reshape(slots_total)[position].reshape(samp_count, picks)
    pair_target = back_target.reshape(slots_total)[position].reshape(samp_count, picks)
    peak_max = jnp.max(pair_max, axis=1)
    norm_sum = jnp.sum(pair_sum * jnp.exp(pair_max - peak_max[:, None]), axis=1)
    log_norm = peak_max + jnp.log(norm_sum)
    sample_loss = log_norm - jnp.sum(pair_target, axis=1)
    send_norm = jnp.zeros((slots_total,), jnp.float32).at[position].set(jnp.repeat(log_norm, picks))
    got_norm = lax.all_to_all(
        send_norm.reshape(owner_count, bucket_dev * slot_depth),
        "own",
        split_axis=0,
        concat_axis=0,
        tiled=True,
    )
    row_norm = (
        got_norm.reshape(owner_count, bucket_dev, slot_depth)
        .transpose(1, 0, 2)
        .reshape(bucket_dev, row_count)
    )
    onehot = (columns == target_col[..., None]).astype(jnp.float32)
    grad_logits = (jnp.exp(logits - row_norm[..., None]) - onehot).astype(jnp.bfloat16)
    grad_weight = jnp.einsum(
        "brc,brd->bcd", grad_logits, received, preferred_element_type=jnp.float32
    ).astype(jnp.bfloat16)
    row_grads = jnp.einsum("brc,bcd->brd", grad_logits, weight, preferred_element_type=jnp.float32)
    send_grads = row_grads.reshape(bucket_dev, owner_count, slot_depth, feature_part).transpose(
        1, 0, 2, 3
    )
    send_grads = send_grads.reshape(owner_count, bucket_dev * slot_depth, feature_part)
    got_grads = lax.all_to_all(send_grads, "own", split_axis=0, concat_axis=0, tiled=True)
    pair_grads = got_grads.reshape(slots_total, feature_part)[position].reshape(
        samp_count, picks, feature_part
    )
    grad_hidden = jnp.sum(pair_grads, axis=1)
    return (sample_loss, grad_hidden, grad_weight)


def choose(hidden, weight, bucket_map, active, label_pick):
    samples, picks = active.shape
    buckets = bucket_map.shape[0]
    depth = 2 * samples * picks // buckets
    fits = (
        weight.shape[0] == 1
        and lax.axis_size("rep") == 4
        and buckets == 8
        and picks == 2
        and samples == 128
        and 2 * depth == samples
        and weight.shape[1] % 512 == 0
        and hidden.shape[1] % 128 == 0
    )
    run = fused if fits else body
    return run(hidden, weight, bucket_map, active, label_pick)


def solution(mesh):
    in_specs = (P("own", "rep"), P("own", None, "rep"), P(), P("own", None), P("own"))
    out_specs = (P("own"), P("own", "rep"), P("own", None, "rep"))
    return jax.shard_map(choose, mesh=mesh, in_specs=in_specs, out_specs=out_specs, check_vma=False)
```
